32 devices in a mesh: groups: 2 (over y), space: 4 (over z), ckpt: 2 (over x), rep: 2 (over core).
Axes of the slice: x: 2, y: 2, z: 4, core: 2. Of those that a mesh axis runs over, the one named last changes fastest.
Arguments:
- adj_disp: bfloat16 [320, 96, 768], P(('groups', 'space', 'rep'), None, 'ckpt'), parts along dimension 0, may hold values from -6 to 6
- adj_vel: bfloat16 [320, 96, 768], P(('groups', 'space', 'rep'), None, 'ckpt'), parts along dimension 0, may hold values from -6 to 6
- tangent_blocks: bfloat16 [320, 96, 768], P(('groups', 'space', 'rep')), parts along dimension 0, may hold values from -0.21875 to 0.21875
- block_cols: int32 [320, 8], P(('groups', 'space', 'rep')), parts along dimension 0, may hold values from 0 to 159, as said below
- inv_mass: float32 [320, 96], P(('groups', 'space', 'rep')), parts along dimension 0, may hold values from 0.25 to 1
- joint_stiff: float32 [320, 96], P(('groups', 'space', 'rep')), parts along dimension 0, may hold values from 0.2 to 1
- contact: int32 [3, 320], P(None, ('groups', 'space', 'rep')), parts along dimension 1, may hold values 0 or 1
- states: float32 [3, 320, 96], P(None, ('groups', 'space', 'rep'), 'ckpt'), parts along dimension 1, may hold values from -4 to 4
Outputs:
- disp_out: float32 [320, 96, 768], P(('groups', 'space', 'rep'), None, 'ckpt'), parts along dimension 0
- vel_out: float32 [320, 96, 768], P(('groups', 'space', 'rep'), None, 'ckpt'), parts along dimension 0
The draws below stay inside these ranges and needn't reach their ends.
There are 2 independent parts, one for each index of `groups`. The reference program is written for one: setup_inputs(seed, part) draws one part's arguments, and reference() takes and returns one part's arrays. A program takes and returns all parts, laid end to end along the dimension named above; each array names one. Nothing has to cross between parts.
Inputs may be any that keep to these rules, and one draw needn't show every extreme that they name: `block_cols`: every block column lies within 4 block rows of its own block row, counted cyclically over the 160 block rows; each block row lists itself and the rows exactly 4 before and after it.
All inputs are finite; a program needn't handle non-finite values. No bound on the sum of `contact` on one device may be relied on, other than what follows from the above.
Results may differ from the reference program's by a relative error of at most 0.015.
Values may be sent and summed in bfloat16 or wider, within the bound.
No kernel may reach another device: no remote copies, remote signals or barrier semaphores. Data moves between devices by JAX's collectives and lax.ppermute only.
A program may use at most 128 MiB of HBM per device.

```python
import math
import jax
import jax.numpy as jnp
from jax import lax

B = 96
NNZ = 8
HB = 4
WINDOW = 3
NB = 160
R = 768


def draw_block_cols(key, part):
    rows = jnp.arange(NB, dtype=jnp.int32)
    spread = jax.random.randint(key, (NB, NNZ - 3), -HB, HB + 1, dtype=jnp.int32)
    fixed = jnp.stack([jnp.zeros((NB,), jnp.int32), jnp.full((NB,), HB, jnp.int32), jnp.full((NB,), -HB, jnp.int32)], axis=1)
    return jnp.mod(rows[:, None] + jnp.concatenate([fixed, spread], axis=1), NB).astype(jnp.int32)


def touch_ends(values, rng, smallest, largest):
    index_at = [jax.random.randint(jax.random.fold_in(rng, axis), (), 0, length) for axis, length in enumerate(values.shape)]
    longest = values.shape.index(max(values.shape))
    neighbour = index_at[:longest] + [(index_at[longest] + 1) % values.shape[longest]] + index_at[longest + 1:]
    return values.at[tuple(index_at)].set(smallest).at[tuple(neighbour)].set(largest)


def block_scale(rng, extent, split, smallest, top_value):
    def one(axis_at, shards_of):
        heights = jax.random.uniform(jax.random.fold_in(jax.random.fold_in(rng, 6), axis_at), (shards_of,), jnp.float32, smallest / len(split), top_value / len(split))
        return jnp.repeat(jnp.exp(heights), extent[axis_at] // shards_of).reshape((-1,) + (1,) * (len(extent) - axis_at - 1))

    gain = one(*split[0])
    for cut in split[1:]:
        gain = gain * one(*cut)
    return gain


def bell_draw(own_key, extent, scale, reach, shards=(), kind=jnp.bfloat16):
    values = jax.random.normal(own_key, extent, jnp.float32) * scale
    if len(shards) > 0:
        values = block_scale(own_key, extent, shards, -0.22, 0.18) * values
    return jnp.clip(values, min=-reach, max=reach).astype(kind)


def setup_inputs(seed: int = 0, part: int = 0) -> dict:
    key_list = jax.random.split(jax.random.key(seed), 9)
    part_keys = jax.random.split(jax.random.fold_in(key_list[8], part), 9)
    return {
        "adj_disp": bell_draw(part_keys[0], (NB, B, R), 1.0, 6.0, ((0, 8), (2, 2))),
        "adj_vel": bell_draw(part_keys[1], (NB, B, R), 1.0, 6.0, ((0, 8), (2, 2))),
        "tangent_blocks": bell_draw(part_keys[2], (NB, B, NNZ * B), (NNZ * B) ** -0.5, 0.21875, ((0, 8),)),
        "block_cols": draw_block_cols(jax.random.fold_in(jax.random.fold_in(key_list[8], part), 71), part),
        "inv_mass": jnp.clip(jnp.exp(math.log(1.0) - 1.3862944 * jax.random.uniform(part_keys[4], (NB, B), jnp.float32) ** block_scale(part_keys[4], (NB, B), ((0, 8),), -0.2, 0.2)), 0.25, 1.0),
        "joint_stiff": jnp.clip(jnp.exp(math.log(1.0) - 1.609438 * jax.random.uniform(part_keys[5], (NB, B), jnp.float32) ** block_scale(part_keys[5], (NB, B), ((0, 8),), -0.2, 0.2)), 0.2, 1.0),
        "contact": touch_ends((jax.random.randint(part_keys[6], (WINDOW, NB), 0, 2) < 1).astype(jnp.int32), jax.random.fold_in(part_keys[6], 1), 0, 1),
        "states": bell_draw(part_keys[7], (WINDOW, NB, B), 1.0, 4.0, ((1, 8), (2, 2)), jnp.float32),
    }


def transposed(packed, tangent_blocks, block_cols):
    count = block_cols.shape[0]
    slots = block_cols.shape[1]
    width = tangent_blocks.shape[1]
    group = math.gcd(count, 16)
    blocks = tangent_blocks.reshape(count // group, group, width, slots * width)
    columns = block_cols.reshape(count // group, group, slots)

    def one_group(item):
        blk, col = item
        picked = jnp.take(packed, col.astype(jnp.int32), axis=0)
        picked = picked.reshape(group, slots * width, packed.shape[2]).astype(jnp.float32)
        return jnp.einsum("bik,bkr->bir", blk.astype(jnp.float32), picked, precision=lax.Precision.HIGHEST)

    result = lax.map(one_group, (blocks, columns))
    return result.reshape(count, width, packed.shape[2])


def reference(adj_disp, adj_vel, tangent_blocks, block_cols, inv_mass, joint_stiff, contact, states):
    disp = adj_disp.astype(jnp.float32)
    vel = adj_vel.astype(jnp.float32)
    accel = jnp.zeros(disp.shape, jnp.float32)
    for back in range(WINDOW):
        step = WINDOW - 1 - back
        total = accel + 0.5 * vel
        packed = (inv_mass[:, :, None] * total).astype(jnp.bfloat16)
        coeff = 3.0 * joint_stiff * contact[step].astype(jnp.float32)[:, None] * states[step] * states[step]
        image = transposed(packed, tangent_blocks, block_cols) + coeff[:, :, None] * packed.astype(jnp.float32)
        disp = disp - image
        accel = 0.5 * disp + 0.5 * vel
        vel = vel + disp
    return disp, vel
```

```python
import functools
import jax
import jax.numpy as jnp
from jax import lax
from jax.experimental import pallas as pl
from jax.experimental.pallas import tpu as pltpu
from jax.sharding import PartitionSpec as P

HB = 4
WINDOW = 3
RING = ("space", "rep")
VMEM_LIMIT = 24 * 1024 * 1024


def ring_pairs(ring):
    inner = [(i, i ^ 1) for i in range(ring)]
    outer = [(i, (i + 1) % ring) for i in range(1, ring, 2)]
    outer = outer + [(b, a) for a, b in outer]
    return inner, outer


def slots_of(cols, r, first, total):
    out = []
    for k in range(cols.shape[1]):
        off = cols[r, k] - (first + r)
        off = jnp.where(off > HB, off - total, off)
        off = jnp.where(off < -HB, off + total, off)
        out.append(r + HB + off)
    return out


def product(blocks, packed, cols, r, first, total):
    picked = jnp.concatenate([packed[p] for p in slots_of(cols, r, first, total)], axis=0)
    return jnp.dot(blocks[r], picked, preferred_element_type=jnp.float32)


def tiled(column, lanes):
    return jnp.concatenate([column] * (lanes // 128), axis=1)


def advance(r, first, total, blocks, packed, cols, coeff, disp_old, vel_old):
    lanes = packed.shape[2]
    image = product(blocks, packed, cols, r, first, total)
    image = image + tiled(coeff[r], lanes) * packed[r + HB].astype(jnp.float32)
    disp = disp_old[r].astype(jnp.float32) - image
    vel = vel_old[r].astype(jnp.float32) + disp
    return disp, vel


def head(vel0, inv_mass, _v, out_b, out_a):
    rows, _, lanes = vel0.shape
    rep = lax.axis_index("rep")
    mass = inv_mass[...].T
    for j in range(HB):
        def packed(r):
            m = jnp.broadcast_to(mass[:, r : r + 1], (mass.shape[0], lanes))
            return m * (0.5 * vel0[r].astype(jnp.float32))
        low, high = packed(j), packed(rows - HB + j)
        out_b[j] = jnp.where(rep == 0, low, high).astype(jnp.bfloat16)
        out_a[j] = jnp.where(rep == 0, high, low).astype(jnp.bfloat16)


def main_first(
    total, pieces, blocks, vel0, disp0, halo, cols, contact, inv_mass, stiff, *rest
):
    shards, rest = rest[:pieces], rest[pieces:]
    _b, _h, now, later, disp, vel, mass_b, coeff, out_a, turned = rest
    rows, _, lanes = vel0.shape
    rep = lax.axis_index("rep")
    me = lax.axis_index("ckpt")
    first = (lax.axis_index("space") * 2 + rep) * rows
    width = shards[0].shape[2]
    mass = inv_mass[...].T
    for r in range(rows):
        m = jnp.broadcast_to(mass[:, r : r + 1], (mass.shape[0], 128))
        mass_b[r] = m
        now[r + HB] = (tiled(m, lanes) * (0.5 * vel0[r].astype(jnp.float32))).astype(
            jnp.bfloat16
        )
    bent = 3.0 * stiff[...].T
    for s in range(WINDOW):
        for j in range(pieces):
            source = lax.rem(me + j, pieces)
            turned[pl.ds(pl.multiple_of(source * width, 8), width), :] = shards[j][s].T
        state = turned[...]
        full = bent * state * state
        for r in range(rows):
            flag = contact[s, r].astype(jnp.float32)
            coeff[s, r] = jnp.broadcast_to(full[:, r : r + 1], (full.shape[0], 128)) * flag
    at_a = (rows + HB) * (1 - rep)
    for j in range(HB):
        now[at_a + j] = halo[j]
    b_start = (rows - HB) * rep
    for j in range(HB):
        disp[b_start + j] = disp0[b_start + j].astype(jnp.float32)
        vel[b_start + j] = vel0[b_start + j].astype(jnp.float32)
    start = HB * (1 - rep)

    def one(i, carry):
        r = start + i
        d, v = advance(r, first, total, blocks, now, cols, coeff.at[WINDOW - 1], disp0, vel0)
        disp[r] = d
        vel[r] = v
        later[r + HB] = (tiled(mass_b[r], lanes) * v).astype(jnp.bfloat16)
        return carry

    lax.fori_loop(0, rows - HB, one, 0, unroll=2)
    a_start = (rows - HB) * (1 - rep)
    for j in range(HB):
        out_a[j] = later[a_start + HB + j]


def middle(total, step, edge, *refs):
    cols = refs[8]
    blocks, now, later, disp, vel, mass_b, coeff, halo, out = refs[9:]
    rows, _, lanes = disp.shape
    rep = lax.axis_index("rep")
    first = (lax.axis_index("space") * 2 + rep) * rows
    side = rep if edge else 1 - rep
    for j in range(HB):
        now[(rows + HB) * side + j] = halo[j]
    if edge:
        start, count = (rows - HB) * rep, HB
    else:
        start, count = HB * (1 - rep), rows - HB

    def one(i, carry):
        r = start + i
        d, v = advance(r, first, total, blocks, now, cols, coeff.at[step], disp, vel)
        disp[r] = d
        vel[r] = v
        p = (tiled(mass_b[r], lanes) * v).astype(jnp.bfloat16)
        later[r + HB] = p
        if edge:
            out[i] = p
        return carry

    lax.fori_loop(0, count, one, 0, unroll=2)
    if not edge:
        for j in range(HB):
            out[j] = later[(rows - HB) * side + HB + j]


def final(total, step, edge, *refs):
    if edge:
        cols = refs[8]
        blocks, now, disp, vel, coeff, halo, disp_out, vel_out, sem = refs[9:]
    else:
        cols = refs[6]
        blocks, now, disp, vel, coeff, halo, disp_out, vel_out, sem = refs[7:]
    rows = disp.shape[0]
    rep = lax.axis_index("rep")
    first = (lax.axis_index("space") * 2 + rep) * rows
    side = rep if edge else 1 - rep
    for j in range(HB):
        now[(rows + HB) * side + j] = halo[j]
    if edge:
        start, count, group = (rows - HB) * rep, HB, 1
    else:
        start, count, group = HB * (1 - rep), rows - HB, HB

    def copies(g):
        at = pl.ds(start + g * group, group)
        return (
            pltpu.make_async_copy(disp.at[at], disp_out.at[at], sem.at[0, g]),
            pltpu.make_async_copy(vel.at[at], vel_out.at[at], sem.at[1, g]),
        )

    for g in range(count // group):
        def one(i, carry):
            r = start + g * group + i
            d, v = advance(r, first, total, blocks, now, cols, coeff.at[step], disp, vel)
            disp[r] = d
            vel[r] = v
            return carry

        lax.fori_loop(0, group, one, 0, unroll=True)
        for c in copies(g):
            c.start()
    for g in range(count // group):
        for c in copies(g):
            c.wait()


def body(adj_disp, adj_vel, tangent_blocks, block_cols, inv_mass, joint_stiff, contact, states):
    rows, width, lanes = adj_disp.shape
    ring = lax.axis_size(RING)
    total = rows * ring
    inner, outer = ring_pairs(ring)
    pieces = lax.axis_size("ckpt")
    f32, bf16 = jnp.float32, jnp.bfloat16
    vm = pl.BlockSpec(memory_space=pltpu.VMEM)
    sm = pl.BlockSpec(memory_space=pltpu.SMEM)
    anyspec = pl.BlockSpec(memory_space=pl.ANY)
    params = pltpu.CompilerParams(vmem_limit_bytes=VMEM_LIMIT)
    like = lambda a: pltpu.VMEM(a.shape, a.dtype)
    edge_t = pltpu.VMEM((HB, width, lanes), bf16)

    shards = [states] + [
        lax.ppermute(states, "ckpt", [((i + j) % pieces, i) for i in range(pieces)])
        for j in range(1, pieces)
    ]

    vel0, out_b, out_a = pl.pallas_call(
        head,
        name="head",
        out_shape=(like(adj_vel), edge_t, edge_t),
        in_specs=[vm] * 2,
        out_specs=(vm,) * 3,
        input_output_aliases={0: 0},
        compiler_params=params,
    )(adj_vel, inv_mass)

    halo_b = lax.ppermute(out_b, RING, outer)
    halo_a = lax.ppermute(out_a, RING, inner)

    ext = pltpu.VMEM((rows + 2 * HB, width, lanes), bf16)
    full = pltpu.VMEM((rows, width, lanes), f32)
    flops = 2 * (rows - HB) * width * tangent_blocks.shape[2] * lanes
    big = pl.CostEstimate(flops=flops, bytes_accessed=6_000_000, transcendentals=0)
    small = pl.CostEstimate(flops=flops * HB // (rows - HB), bytes_accessed=1_000_000, transcendentals=0)
    blocks, _, now, later, disp, vel, mass_b, coeff, out_a = pl.pallas_call(
        functools.partial(main_first, total, pieces),
        name="main_first",
        out_shape=(
            like(tangent_blocks), edge_t, ext, ext, full, full,
            pltpu.VMEM((rows, width, 128), f32),
            pltpu.VMEM((WINDOW, rows, width, 128), f32),
            edge_t,
        ),
        in_specs=[vm] * 4 + [sm] * 2 + [vm] * (2 + pieces),
        out_specs=(vm,) * 9,
        scratch_shapes=[pltpu.VMEM((width, rows), f32)],
        input_output_aliases={0: 0, 3: 1},
        compiler_params=params,
        cost_estimate=big,
    )(tangent_blocks, vel0, adj_disp, halo_a, block_cols, contact, inv_mass, joint_stiff, *shards)

    def run_middle(step, edge, held, halo):
        return pl.pallas_call(
            functools.partial(middle, total, step, edge),
            name=("edge" if edge else "main") + str(step),
            out_shape=tuple(like(a) for a in held) + (edge_t, edge_t),
            in_specs=[vm] * 8 + [sm],
            out_specs=(vm,) * 9,
            input_output_aliases={i: i for i in range(8)},
            compiler_params=params,
            cost_estimate=small if edge else big,
        )(*held, halo, block_cols)

    step = WINDOW - 1
    held = [blocks, now, later, disp, vel, mass_b, coeff]
    while step > 0:
        next_a = lax.ppermute(out_a, RING, inner)
        *held, _, out_b = run_middle(step, True, held, halo_b)
        halo_b = lax.ppermute(out_b, RING, outer)
        halo_a = next_a
        step -= 1
        held[1], held[2] = held[2], held[1]
        if step > 0:
            *held, _, out_a = run_middle(step, False, held, halo_a)

    blocks, now, later, disp, vel, mass_b, coeff = held
    shape = jax.ShapeDtypeStruct((rows, width, lanes), f32)
    held = [blocks, now, disp, vel, coeff]
    *held, _, disp_out, vel_out = pl.pallas_call(
        functools.partial(final, total, 0, False),
        name="main_last",
        out_shape=tuple(like(a) for a in held) + (edge_t, shape, shape),
        in_specs=[vm] * 6 + [sm],
        out_specs=(vm,) * 6 + (anyspec,) * 2,
        scratch_shapes=[pltpu.SemaphoreType.DMA((2, rows // HB - 1))],
        input_output_aliases={i: i for i in range(6)},
        compiler_params=params,
        cost_estimate=big,
    )(*held, halo_a, block_cols)
    out = pl.pallas_call(
        functools.partial(final, total, 0, True),
        name="edge_last",
        out_shape=tuple(like(a) for a in held) + (edge_t, shape, shape),
        in_specs=[vm] * 6 + [anyspec] * 2 + [sm],
        out_specs=(vm,) * 6 + (anyspec,) * 2,
        scratch_shapes=[pltpu.SemaphoreType.DMA((2, HB))],
        input_output_aliases={i: i for i in range(8)},
        compiler_params=params,
        cost_estimate=small,
    )(*held, halo_b, disp_out, vel_out, block_cols)
    return out[-2], out[-1]


def solution(mesh):
    placed = (
        P(("groups", "space", "rep"), None, "ckpt"),
        P(("groups", "space", "rep"), None, "ckpt"),
        P(("groups", "space", "rep"), None, None),
        P(("groups", "space", "rep"), None),
        P(("groups", "space", "rep"), None),
        P(("groups", "space", "rep"), None),
        P(None, ("groups", "space", "rep")),
        P(None, ("groups", "space", "rep"), "ckpt"),
    )
    return jax.shard_map(
        body,
        mesh=mesh,
        in_specs=placed,
        out_specs=(
            P(("groups", "space", "rep"), None, "ckpt"),
            P(("groups", "space", "rep"), None, "ckpt"),
        ),
        check_vma=False,
    )
```

```python
import functools
import jax
import jax.numpy as jnp
from jax import lax
from jax.experimental import pallas as pl
from jax.experimental.pallas import tpu as pltpu
from jax.sharding import PartitionSpec as P

HB = 4
WINDOW = 3
RING = ("space", "rep")
VMEM_LIMIT = 24 * 1024 * 1024


def ring_pairs(ring):
    inner = [(i, i ^ 1) for i in range(ring)]
    outer = [(i, (i + 1) % ring) for i in range(1, ring, 2)]
    outer = outer + [(b, a) for a, b in outer]
    return inner, outer


def product(blocks, packed, place, r):
    slots = blocks.shape[2] // blocks.shape[1]
    picked = jnp.concatenate([packed[place[k, r]] for k in range(slots)], axis=0)
    return jnp.dot(blocks[r], picked, preferred_element_type=jnp.float32)


def tiled(column, lanes):
    return jnp.concatenate([column] * (lanes // 128), axis=1)


def spread(matrix, r, lanes):
    return jnp.broadcast_to(matrix[:, r : r + 1], (matrix.shape[0], lanes))


def each(count, one):
    def run(i, carry):
        one(i)
        return carry

    lax.fori_loop(0, count, run, 0, unroll=True)


def begin(copies):
    for c in copies:
        c.start()
    return copies


def end(copies):
    for c in copies:
        c.wait()


def head(vel0, inv_mass, out_b, out_a, low, high, mass, sem):
    rows, _, lanes = vel0.shape
    end(
        begin(
            [
                pltpu.make_async_copy(inv_mass, mass, sem.at[0]),
                pltpu.make_async_copy(vel0.at[pl.ds(0, HB)], low, sem.at[1]),
                pltpu.make_async_copy(vel0.at[pl.ds(rows - HB, HB)], high, sem.at[2]),
            ]
        )
    )
    rep = lax.axis_index("rep")
    turned = mass[...].T
    for j in range(HB):
        p = spread(turned, j, lanes) * (0.5 * low[j].astype(jnp.float32))
        q = spread(turned, rows - HB + j, lanes) * (0.5 * high[j].astype(jnp.float32))
        out_b[j] = jnp.where(rep == 0, p, q).astype(jnp.bfloat16)
        out_a[j] = jnp.where(rep == 0, q, p).astype(jnp.bfloat16)


def first_products(
    total, blocks_in, vel0_in, disp0_in, inv_mass, halo, cols,
    blocks, now, disp, vel, mass_b, place, vel0, disp0, mass, sem,
):
    rows, _, lanes = vel0.shape
    slots = cols.shape[0]
    begin(
        [
            pltpu.make_async_copy(inv_mass, mass, sem.at[0]),
            pltpu.make_async_copy(vel0_in, vel0, sem.at[1]),
            pltpu.make_async_copy(disp0_in, disp0, sem.at[2]),
            pltpu.make_async_copy(blocks_in, blocks, sem.at[3]),
        ]
    )
    rep = lax.axis_index("rep")
    first = (lax.axis_index("space") * 2 + rep) * rows
    for r in range(rows):
        for k in range(slots):
            off = cols[k, r] - (first + r)
            off = jnp.where(off > HB, off - total, off)
            off = jnp.where(off < -HB, off + total, off)
            place[k, r] = r + HB + off
    pltpu.make_async_copy(inv_mass, mass, sem.at[0]).wait()
    turned = mass[...].T
    for r in range(rows):
        mass_b[r] = spread(turned, r, 128)
    pltpu.make_async_copy(vel0_in, vel0, sem.at[1]).wait()
    for r in range(rows):
        v = vel0[r].astype(jnp.float32)
        vel[r] = v
        now[r + HB] = (tiled(mass_b[r], lanes) * (0.5 * v)).astype(jnp.bfloat16)
    at_a = (rows + HB) * (1 - rep)
    for j in range(HB):
        now[at_a + j] = halo[j]
    pltpu.make_async_copy(disp0_in, disp0, sem.at[2]).wait()
    b_start = (rows - HB) * rep
    for j in range(HB):
        disp[b_start + j] = disp0[b_start + j].astype(jnp.float32)
    pltpu.make_async_copy(blocks_in, blocks, sem.at[3]).wait()
    start = HB * (1 - rep)

    def one(i):
        r = start + i
        disp[r] = disp0[r].astype(jnp.float32) - product(blocks, now, place, r)

    each(rows - HB, one)


def first_rows(start, count, now, later, disp, vel, mass_b, coeff):
    lanes = disp.shape[2]

    def one(i):
        r = start + i
        d = disp[r] - tiled(coeff[WINDOW - 1, r], lanes) * now[r + HB].astype(jnp.float32)
        v = vel[r] + d
        disp[r] = d
        vel[r] = v
        later[r + HB] = (tiled(mass_b[r], lanes) * v).astype(jnp.bfloat16)

    each(count, one)


def coefficients(pieces, *refs):
    stiff_in, contact_in, mine = refs[4:7]
    now, disp, vel, mass_b, *others = refs[6 + pieces : 9 + 2 * pieces]
    later, coeff, out_a, stiff, contact, shard, turned, sem = refs[9 + 2 * pieces :]
    rows, width = stiff.shape
    part = width // pieces
    end(
        begin(
            [
                pltpu.make_async_copy(stiff_in, stiff, sem.at[0]),
                pltpu.make_async_copy(contact_in, contact, sem.at[1]),
                pltpu.make_async_copy(mine, shard, sem.at[2]),
            ]
        )
    )
    me = lax.axis_index("ckpt")
    bent = 3.0 * stiff[...].T
    for s in range(WINDOW):
        for j, piece in enumerate((shard,) + tuple(others)):
            source = lax.rem(me + j, pieces)
            turned[s, pl.ds(pl.multiple_of(source * part, 8), part), :] = piece[s].T
        state = turned[s]
        full = bent * state * state
        for r in range(rows):
            coeff[s, r] = spread(full, r, 128) * contact[s, r].astype(jnp.float32)
    start = (rows - HB) * (1 - lax.axis_index("rep"))
    first_rows(start, HB, now, later, disp, vel, mass_b, coeff)
    for j in range(HB):
        out_a[j] = later[start + HB + j]


def first_update(*refs):
    now, later, disp, vel, mass_b, coeff = refs[6:]
    first_rows(HB, disp.shape[0] - 2 * HB, now, later, disp, vel, mass_b, coeff)


def advance(step, r, blocks, now, place, coeff, disp, vel):
    lanes = now.shape[2]
    image = product(blocks, now, place, r)
    image = image + tiled(coeff[step, r], lanes) * now[r + HB].astype(jnp.float32)
    d = disp[r] - image
    v = vel[r] + d
    disp[r] = d
    vel[r] = v
    return v


def extent(rows, edge, rep):
    if edge:
        return rep, (rows - HB) * rep, HB
    return 1 - rep, HB * (1 - rep), rows - HB


def middle(step, edge, *refs):
    place, blocks, now, disp, vel, mass_b, coeff, halo, later, out = refs[-10:]
    rows, _, lanes = disp.shape
    side, start, count = extent(rows, edge, lax.axis_index("rep"))
    for j in range(HB):
        now[(rows + HB) * side + j] = halo[j]

    def one(i):
        r = start + i
        v = advance(step, r, blocks, now, place, coeff, disp, vel)
        p = (tiled(mass_b[r], lanes) * v).astype(jnp.bfloat16)
        later[r + HB] = p
        if edge:
            out[i] = p

    each(count, one)
    if not edge:
        for j in range(HB):
            out[j] = later[(rows - HB) * side + HB + j]


def final(step, edge, *refs):
    place = refs[8 if edge else 6]
    blocks, now, disp, vel, coeff, halo, disp_out, vel_out, sem = refs[(9 if edge else 7) :]
    rows = disp.shape[0]
    side, start, count = extent(rows, edge, lax.axis_index("rep"))
    group = 1 if edge else HB
    for j in range(HB):
        now[(rows + HB) * side + j] = halo[j]

    def copies(g):
        at = pl.ds(start + g * group, group)
        return [
            pltpu.make_async_copy(disp.at[at], disp_out.at[at], sem.at[0, g]),
            pltpu.make_async_copy(vel.at[at], vel_out.at[at], sem.at[1, g]),
        ]

    for g in range(count // group):
        each(group, lambda i: advance(step, start + g * group + i, blocks, now, place, coeff, disp, vel))
        begin(copies(g))
    for g in range(count // group):
        end(copies(g))


def body(adj_disp, adj_vel, tangent_blocks, block_cols, inv_mass, joint_stiff, contact, states):
    rows, width, lanes = adj_disp.shape
    ring = lax.axis_size(RING)
    total = rows * ring
    inner, outer = ring_pairs(ring)
    pieces = lax.axis_size("ckpt")
    f32, bf16 = jnp.float32, jnp.bfloat16
    vm = pl.BlockSpec(memory_space=pltpu.VMEM)
    sm = pl.BlockSpec(memory_space=pltpu.SMEM)
    hbm = pl.BlockSpec(memory_space=pltpu.HBM)
    params = pltpu.CompilerParams(vmem_limit_bytes=VMEM_LIMIT)
    like = lambda a: pltpu.VMEM(a.shape, a.dtype)
    edge_t = pltpu.VMEM((HB, width, lanes), bf16)
    ext = pltpu.VMEM((rows + 2 * HB, width, lanes), bf16)
    full = pltpu.VMEM((rows, width, lanes), f32)
    dma = pltpu.SemaphoreType.DMA
    flops = 2 * (rows - HB) * width * tangent_blocks.shape[2] * lanes
    big = pl.CostEstimate(flops=flops // 64, bytes_accessed=100_000, transcendentals=0)
    small = pl.CostEstimate(flops=flops // 256, bytes_accessed=25_000, transcendentals=0)
    adj_disp, adj_vel, tangent_blocks, cols, inv_mass, joint_stiff, contact, mine = (
        pltpu.with_memory_space_constraint(a, pltpu.HBM)
        for a in (
            adj_disp, adj_vel, tangent_blocks, block_cols.T, inv_mass, joint_stiff, contact, states
        )
    )

    out_b, out_a = pl.pallas_call(
        head,
        name="head",
        out_shape=(edge_t, edge_t),
        in_specs=[hbm] * 2,
        out_specs=(vm,) * 2,
        scratch_shapes=[edge_t, edge_t, pltpu.VMEM((rows, width), f32), dma((3,))],
        compiler_params=params,
    )(adj_vel, inv_mass)

    states_late, out_a = lax.optimization_barrier((states, out_a))
    halo_a = lax.ppermute(out_a, RING, inner)
    halo_b = lax.ppermute(out_b, RING, outer)
    shards = [mine] + [
        lax.ppermute(states_late, "ckpt", [((i + j) % pieces, i) for i in range(pieces)])
        for j in range(1, pieces)
    ]

    blocks, now, disp, vel, mass_b, place = pl.pallas_call(
        functools.partial(first_products, total),
        name="first_products",
        out_shape=(
            like(tangent_blocks), ext, full, full,
            pltpu.VMEM((rows, width, 128), f32),
            jax.ShapeDtypeStruct(cols.shape, jnp.int32),
        ),
        in_specs=[hbm] * 4 + [vm, sm],
        out_specs=(vm,) * 5 + (sm,),
        scratch_shapes=[like(adj_vel), like(adj_disp), pltpu.VMEM((rows, width), f32), dma((4,))],
        compiler_params=params,
        cost_estimate=big,
    )(tangent_blocks, adj_vel, adj_disp, inv_mass, halo_a, cols)

    now, disp, vel, mass_b, *_, later, coeff, out_a = pl.pallas_call(
        functools.partial(coefficients, pieces),
        name="coefficients",
        out_shape=(like(now), like(disp), like(vel), like(mass_b))
        + tuple(like(a) for a in shards[1:])
        + (ext, pltpu.VMEM((WINDOW, rows, width, 128), f32), edge_t),
        in_specs=[vm] * 4 + [hbm] * 3 + [vm] * (pieces - 1),
        out_specs=(vm,) * (pieces + 6),
        input_output_aliases={i: i for i in range(4)} | {6 + j: 3 + j for j in range(1, pieces)},
        scratch_shapes=[
            pltpu.VMEM((rows, width), f32),
            pltpu.SMEM(contact.shape, jnp.int32),
            pltpu.VMEM(states.shape, f32),
            pltpu.VMEM((WINDOW, width, rows), f32),
            dma((3,)),
        ],
        compiler_params=params,
        cost_estimate=small,
    )(now, disp, vel, mass_b, joint_stiff, contact, *shards)

    def run_middle(step, edge, held, halo, later):
        given = list(held) + [halo, later]
        *out, edge_rows = pl.pallas_call(
            functools.partial(middle, step, edge),
            name=("edge" if edge else "main") + str(step),
            out_shape=tuple(like(a) for a in held) + (edge_t, ext, edge_t),
            in_specs=[vm] * len(given) + [sm],
            out_specs=(vm,) * 9,
            input_output_aliases={i: i for i in range(len(given))},
            compiler_params=params,
            cost_estimate=small if edge else big,
        )(*given, place)
        return out[:6], out[7], edge_rows

    held = [blocks, now, disp, vel, mass_b, coeff]
    step = WINDOW - 1
    halo_a = lax.ppermute(out_a, RING, inner)
    held, later, out_b = run_middle(step, True, held, halo_b, later)
    halo_b = lax.ppermute(out_b, RING, outer)
    blocks, now, disp, vel, mass_b, coeff = held
    now, later, disp, vel, mass_b, coeff = pl.pallas_call(
        first_update,
        name="first_update",
        out_shape=(ext, ext, full, full, like(mass_b), like(coeff)),
        in_specs=[vm] * 6,
        out_specs=(vm,) * 6,
        input_output_aliases={i: i for i in range(6)},
        compiler_params=params,
        cost_estimate=small,
    )(now, later, disp, vel, mass_b, coeff)

    step -= 1
    while step > 0:
        held = [blocks, later, disp, vel, mass_b, coeff]
        held, later, out_a = run_middle(step, False, held, halo_a, now)
        halo_a = lax.ppermute(out_a, RING, inner)
        held, later, out_b = run_middle(step, True, held, halo_b, later)
        halo_b = lax.ppermute(out_b, RING, outer)
        blocks, now, disp, vel, mass_b, coeff = held
        step -= 1

    shape = jax.ShapeDtypeStruct((rows, width, lanes), f32)
    held = [blocks, later, disp, vel, coeff]
    *held, _, disp_out, vel_out = pl.pallas_call(
        functools.partial(final, 0, False),
        name="main_last",
        out_shape=tuple(like(a) for a in held) + (edge_t, shape, shape),
        in_specs=[vm] * 6 + [sm],
        out_specs=(vm,) * 6 + (hbm,) * 2,
        scratch_shapes=[dma((2, rows // HB - 1))],
        input_output_aliases={i: i for i in range(6)},
        compiler_params=params,
        cost_estimate=big,
    )(*held, halo_a, place)
    out = pl.pallas_call(
        functools.partial(final, 0, True),
        name="edge_last",
        out_shape=tuple(like(a) for a in held) + (edge_t, shape, shape),
        in_specs=[vm] * 6 + [hbm] * 2 + [sm],
        out_specs=(vm,) * 6 + (hbm,) * 2,
        scratch_shapes=[dma((2, HB))],
        input_output_aliases={i: i for i in range(8)},
        compiler_params=params,
        cost_estimate=small,
    )(*held, halo_b, disp_out, vel_out, place)
    return out[-2], out[-1]


def solution(mesh):
    placed = (
        P(("groups", "space", "rep"), None, "ckpt"),
        P(("groups", "space", "rep"), None, "ckpt"),
        P(("groups", "space", "rep"), None, None),
        P(("groups", "space", "rep"), None),
        P(("groups", "space", "rep"), None),
        P(("groups", "space", "rep"), None),
        P(None, ("groups", "space", "rep")),
        P(None, ("groups", "space", "rep"), "ckpt"),
    )
    return jax.shard_map(
        body,
        mesh=mesh,
        in_specs=placed,
        out_specs=(
            P(("groups", "space", "rep"), None, "ckpt"),
            P(("groups", "space", "rep"), None, "ckpt"),
        ),
        check_vma=False,
    )
```

```python
import functools
import jax
import jax.numpy as jnp
from jax import lax
from jax.experimental import pallas as pl
from jax.experimental.pallas import tpu as pltpu
from jax.sharding import PartitionSpec as P

HB = 4
WINDOW = 3
RING = ("space", "rep")
VMEM_LIMIT = 24 * 1024 * 1024


def ring_pairs(ring):
    inner = [(i, i ^ 1) for i in range(ring)]
    outer = [(i, (i + 1) % ring) for i in range(1, ring, 2)]
    outer = outer + [(b, a) for a, b in outer]
    return inner, outer


def product(blocks, packed, place, r):
    slots = blocks.shape[2] // blocks.shape[1]
    picked = jnp.concatenate([packed[place[k, r]] for k in range(slots)], axis=0)
    return jnp.dot(blocks[r], picked, preferred_element_type=jnp.float32)


def tiled(column, lanes):
    return jnp.concatenate([column] * (lanes // 128), axis=1)


def spread(matrix, r, lanes):
    return jnp.broadcast_to(matrix[:, r : r + 1], (matrix.shape[0], lanes))


def each(count, one):
    def run(i, carry):
        one(i)
        return carry

    lax.fori_loop(0, count, run, 0, unroll=True)


def begin(copies):
    for c in copies:
        c.start()
    return copies


def end(copies):
    for c in copies:
        c.wait()


def head(vel0, inv_mass, out_b, out_a, low, high, mass, sem):
    rows, _, lanes = vel0.shape
    end(
        begin(
            [
                pltpu.make_async_copy(inv_mass, mass, sem.at[0]),
                pltpu.make_async_copy(vel0.at[pl.ds(0, HB)], low, sem.at[1]),
                pltpu.make_async_copy(vel0.at[pl.ds(rows - HB, HB)], high, sem.at[2]),
            ]
        )
    )
    rep = lax.axis_index("rep")
    turned = mass[...].T
    for j in range(HB):
        p = spread(turned, j, lanes) * (0.5 * low[j].astype(jnp.float32))
        q = spread(turned, rows - HB + j, lanes) * (0.5 * high[j].astype(jnp.float32))
        out_b[j] = jnp.where(rep == 0, p, q).astype(jnp.bfloat16)
        out_a[j] = jnp.where(rep == 0, q, p).astype(jnp.bfloat16)


def load_all(
    total, pieces, blocks_in, vel0_in, disp0_in, inv_mass, stiff_in, contact_in, mine, halo, cols,
    blocks, disp0, now, disp, vel, mass_b, bent, turned, place, vel0, mass, stiff, contact, shard, sem,
):
    rows, _, lanes = vel0.shape
    slots = cols.shape[0]
    rep = lax.axis_index("rep")
    a_start = (rows - HB) * (1 - rep)
    b_start = (rows - HB) * rep
    at = pl.ds(a_start, HB)
    small = begin(
        [
            pltpu.make_async_copy(inv_mass, mass, sem.at[0]),
            pltpu.make_async_copy(stiff_in, stiff, sem.at[1]),
            pltpu.make_async_copy(contact_in, contact, sem.at[2]),
            pltpu.make_async_copy(mine, shard, sem.at[3]),
        ]
    )
    get_vel = begin([pltpu.make_async_copy(vel0_in, vel0, sem.at[4])])
    get_rest = begin(
        [
            pltpu.make_async_copy(blocks_in, blocks, sem.at[5]),
            pltpu.make_async_copy(disp0_in, disp0, sem.at[6]),
        ]
    )
    first = (lax.axis_index("space") * 2 + rep) * rows
    for r in range(rows):
        for k in range(slots):
            off = cols[k, r] - (first + r)
            off = jnp.where(off > HB, off - total, off)
            off = jnp.where(off < -HB, off + total, off)
            place[k, r] = r + HB + off
    now[rows + 2 * HB] = jnp.zeros(now.shape[1:], now.dtype)
    side = (rows + HB) * (1 - rep)
    for j in range(HB):
        now[side + j] = halo[j]
    end(small)
    upright = mass[...].T
    for r in range(rows):
        mass_b[r] = spread(upright, r, 128)
    part = shard.shape[2]
    home = pl.ds(pl.multiple_of(lax.axis_index("ckpt") * part, 8), part)
    stiff3 = 3.0 * stiff[...].T
    for s in range(WINDOW):
        bent[s] = stiff3 * contact[s : s + 1, :].astype(jnp.float32)
        turned[s, home, :] = shard[s].T
    end(get_vel)
    for r in range(rows):
        v = vel0[r].astype(jnp.float32)
        vel[r] = v
        now[r + HB] = (tiled(mass_b[r], lanes) * (0.5 * v)).astype(jnp.bfloat16)
    end(get_rest)
    for j in range(HB):
        disp[b_start + j] = disp0[b_start + j].astype(jnp.float32)

    def one(i):
        r = a_start + i
        disp[r] = disp0[r].astype(jnp.float32) - product(blocks, now, place, r)

    each(HB, one)


def finish_row(r, image, now, later, disp, vel, mass_b):
    d = disp[r] - image
    v = vel[r] + d
    disp[r] = d
    vel[r] = v
    if later is not None:
        p = (tiled(mass_b[r], disp.shape[2]) * v).astype(jnp.bfloat16)
        later[r + HB] = p
        return p


def joint(step, r, now, coeff):
    return tiled(coeff[step, r], now.shape[2]) * now[r + HB].astype(jnp.float32)


def coefficients(pieces, *refs):
    now, disp, vel, mass_b, bent, turned, *others = refs[5 + pieces : 10 + 2 * pieces]
    later, coeff, out_a = refs[10 + 2 * pieces :]
    rows, _, lanes = disp.shape
    part = turned.shape[1] // pieces
    me = lax.axis_index("ckpt")
    last = WINDOW - 1
    for s in range(WINDOW):
        for j, piece in enumerate(others):
            source = lax.rem(me + 1 + j, pieces)
            turned[s, pl.ds(pl.multiple_of(source * part, 8), part), :] = piece[s].T
        turned[s] = bent[s] * turned[s] * turned[s]
    full = turned[last]
    for r in range(rows):
        coeff[last, r] = spread(full, r, 128)
    later[rows + 2 * HB] = jnp.zeros(later.shape[1:], later.dtype)
    start = (rows - HB) * (1 - lax.axis_index("rep"))

    def one(i):
        r = start + i
        out_a[i] = finish_row(r, joint(last, r, now, coeff), now, later, disp, vel, mass_b)

    each(HB, one)


def first_edge(*refs):
    place, blocks, now, disp, vel, mass_b, coeff, halo, later, out = refs[-10:]
    rows = disp.shape[0]
    rep = lax.axis_index("rep")
    for j in range(HB):
        now[(rows + HB) * rep + j] = halo[j]
    start = (rows - HB) * rep

    def one(i):
        r = start + i
        image = product(blocks, now, place, r) + joint(WINDOW - 1, r, now, coeff)
        out[i] = finish_row(r, image, now, later, disp, vel, mass_b)

    each(HB, one)


def first_interior(*refs):
    place, blocks, disp0, now, later, disp, vel, mass_b, turned, coeff, dense, wide = refs[-12:]
    rows, width, lanes = disp.shape
    slots = blocks.shape[2] // width

    def one(i):
        r = HB + i
        disp[r] = disp0[r].astype(jnp.float32)
        image = product(blocks, now, place, r) + joint(WINDOW - 1, r, now, coeff)
        finish_row(r, image, now, later, disp, vel, mass_b)

    each(rows - 2 * HB, one)
    for s in range(WINDOW - 1):
        full = turned[s]
        for r in range(rows):
            coeff[s, r] = spread(full, r, 128)
    rep = lax.axis_index("rep")
    wide[...] = jnp.zeros_like(wide)
    for i in range(HB):
        r = (rows - HB) * rep + i
        block = blocks[r].astype(jnp.float32)
        for k in range(slots):
            j = place[k, r] - (rows + HB) * rep
            inside = jnp.logical_and(j >= 0, j < HB)

            @pl.when(inside)
            def _():
                at = pl.ds(i * width, width)
                wide[j, at, pl.ds(0, width)] += block[:, k * width : (k + 1) * width]

    dense[...] = jnp.concatenate([wide[j, :, :width] for j in range(HB)], axis=1).astype(
        jnp.bfloat16
    )


def near_part(step, i, blocks, now, place, coeff, disp):
    rows = disp.shape[0]
    rep = lax.axis_index("rep")
    r = (rows - HB) * rep + i
    low = (rows + HB) * rep
    slots = blocks.shape[2] // blocks.shape[1]
    picked = []
    for k in range(slots):
        p = place[k, r]
        inside = jnp.logical_and(p >= low, p < low + HB)
        picked.append(now[jnp.where(inside, rows + 2 * HB, p)])
    image = jnp.dot(
        blocks[r], jnp.concatenate(picked, axis=0), preferred_element_type=jnp.float32
    )
    disp[r] = disp[r] - (image + joint(step, r, now, coeff))


def main_rows(step, *refs):
    place, blocks, now, disp, vel, mass_b, coeff, halo, later, out = refs[-10:]
    rows = disp.shape[0]
    side = 1 - lax.axis_index("rep")
    for j in range(HB):
        now[(rows + HB) * side + j] = halo[j]
    start = HB * side

    def one(i):
        r = start + i
        image = product(blocks, now, place, r) + joint(step, r, now, coeff)
        finish_row(r, image, now, later, disp, vel, mass_b)

    each(rows - HB, one)
    for j in range(HB):
        out[j] = later[(rows - HB) * side + HB + j]
    each(HB, lambda i: near_part(step, i, blocks, now, place, coeff, disp))


def far_part(dense, halo):
    rows, width, lanes = halo.shape
    return jnp.dot(
        dense[...], halo[...].reshape(rows * width, lanes), preferred_element_type=jnp.float32
    )


def edge_rows(*refs):
    dense, disp, vel, mass_b, halo, later, out = refs[-7:]
    rows, width, _ = disp.shape
    image = far_part(dense, halo)
    start = (rows - HB) * lax.axis_index("rep")
    for i in range(HB):
        part = image[i * width : (i + 1) * width]
        out[i] = finish_row(start + i, part, None, later, disp, vel, mass_b)


def row_copies(disp, vel, disp_out, vel_out, sem, start, count, g):
    at = pl.ds(start, count)
    return [
        pltpu.make_async_copy(disp.at[at], disp_out.at[at], sem.at[0, g]),
        pltpu.make_async_copy(vel.at[at], vel_out.at[at], sem.at[1, g]),
    ]


def main_last(*refs):
    place, blocks, now, disp, vel, coeff, halo, disp_out, vel_out, sem = refs[-10:]
    rows = disp.shape[0]
    side = 1 - lax.axis_index("rep")
    for j in range(HB):
        now[(rows + HB) * side + j] = halo[j]
    sent = []
    for g in range(rows // HB - 1):
        start = HB * side + g * HB

        def one(i):
            r = start + i
            image = product(blocks, now, place, r) + joint(0, r, now, coeff)
            finish_row(r, image, now, None, disp, vel, None)

        each(HB, one)
        sent += begin(row_copies(disp, vel, disp_out, vel_out, sem, start, HB, g))
    each(HB, lambda i: near_part(0, i, blocks, now, place, coeff, disp))
    end(sent)


def edge_last(*refs):
    dense, disp, vel, halo, disp_out, vel_out, sem = refs[-7:]
    rows, width, _ = disp.shape
    image = far_part(dense, halo)
    start = (rows - HB) * lax.axis_index("rep")
    sent = []
    for i in range(HB):
        finish_row(start + i, image[i * width : (i + 1) * width], None, None, disp, vel, None)
        sent += begin(row_copies(disp, vel, disp_out, vel_out, sem, start + i, 1, i))
    end(sent)


def body(adj_disp, adj_vel, tangent_blocks, block_cols, inv_mass, joint_stiff, contact, states):
    rows, width, lanes = adj_disp.shape
    ring = lax.axis_size(RING)
    total = rows * ring
    inner, outer = ring_pairs(ring)
    pieces = lax.axis_size("ckpt")
    f32, bf16 = jnp.float32, jnp.bfloat16
    vm = pl.BlockSpec(memory_space=pltpu.VMEM)
    sm = pl.BlockSpec(memory_space=pltpu.SMEM)
    hbm = pl.BlockSpec(memory_space=pltpu.HBM)
    like = lambda a: pltpu.VMEM(a.shape, a.dtype)
    edge_t = pltpu.VMEM((HB, width, lanes), bf16)
    ext = pltpu.VMEM((rows + 2 * HB + 1, width, lanes), bf16)
    full = pltpu.VMEM((rows, width, lanes), f32)
    table = pltpu.VMEM((rows, width), f32)
    upright = pltpu.VMEM((WINDOW, width, rows), f32)
    dma = pltpu.SemaphoreType.DMA
    flops = 2 * (rows - HB) * width * tangent_blocks.shape[2] * lanes
    big = pl.CostEstimate(flops=flops // 64, bytes_accessed=100_000, transcendentals=0)
    small = pl.CostEstimate(flops=flops // 256, bytes_accessed=25_000, transcendentals=0)
    adj_disp, adj_vel, tangent_blocks, cols, inv_mass, joint_stiff, contact, mine = (
        pltpu.with_memory_space_constraint(a, pltpu.HBM)
        for a in (
            adj_disp, adj_vel, tangent_blocks, block_cols.T, inv_mass, joint_stiff, contact, states
        )
    )

    def call(kernel, name, held, given, specs, made, made_specs, scratch=(), cost=small):
        return pl.pallas_call(
            kernel,
            name=name,
            out_shape=tuple(like(a) for a in held) + tuple(made),
            in_specs=[vm] * len(held) + list(specs),
            out_specs=(vm,) * len(held) + tuple(made_specs),
            input_output_aliases={i: i for i in range(len(held))},
            scratch_shapes=list(scratch),
            compiler_params=pltpu.CompilerParams(vmem_limit_bytes=VMEM_LIMIT),
            cost_estimate=cost,
        )(*held, *given)

    out_b, out_a = call(
        head, "head", [], [adj_vel, inv_mass], [hbm] * 2, [edge_t] * 2, [vm] * 2,
        [edge_t, edge_t, table, dma((3,))],
    )
    states_late, out_a = lax.optimization_barrier((states, out_a))
    halo_a = lax.ppermute(out_a, RING, inner)
    halo_b = lax.ppermute(out_b, RING, outer)
    others = [
        lax.ppermute(states_late, "ckpt", [((i + j) % pieces, i) for i in range(pieces)])
        for j in range(1, pieces)
    ]

    _, blocks, disp0, now, disp, vel, mass_b, bent, turned, place = pl.pallas_call(
        lambda *refs: load_all(
            total, pieces, *refs[1:8], refs[0], refs[8], *refs[10:]
        ),
        name="load_all",
        out_shape=(
            edge_t, like(tangent_blocks), like(adj_disp), ext, full, full,
            pltpu.VMEM((rows, width, 128), f32), upright, upright,
            jax.ShapeDtypeStruct(cols.shape, jnp.int32),
        ),
        in_specs=[vm] + [hbm] * 7 + [sm],
        out_specs=(vm,) * 9 + (sm,),
        input_output_aliases={0: 0},
        scratch_shapes=[
            like(adj_vel), table, table, pltpu.VMEM(contact.shape, jnp.int32),
            pltpu.VMEM(states.shape, f32), dma((7,)),
        ],
        compiler_params=pltpu.CompilerParams(vmem_limit_bytes=VMEM_LIMIT),
        cost_estimate=big,
    )(halo_a, tangent_blocks, adj_vel, adj_disp, inv_mass, joint_stiff, contact, mine, cols)

    now, disp, vel, mass_b, _, turned, *_, later, coeff, out_a = call(
        functools.partial(coefficients, pieces), "coefficients",
        [now, disp, vel, mass_b, bent, turned] + others, [], [],
        [ext, pltpu.VMEM((WINDOW, rows, width, 128), f32), edge_t], [vm] * 3,
    )
    halo_a = lax.ppermute(out_a, RING, inner)
    blocks, now, disp, vel, mass_b, coeff, _, later, out_b = call(
        first_edge, "first_edge",
        [blocks, now, disp, vel, mass_b, coeff, halo_b, later], [place], [sm], [edge_t], [vm],
    )
    halo_b = lax.ppermute(out_b, RING, outer)
    blocks, _, now, later, disp, vel, mass_b, _, coeff, dense = call(
        first_interior, "first_interior",
        [blocks, disp0, now, later, disp, vel, mass_b, turned, coeff], [place], [sm],
        [pltpu.VMEM((HB * width, HB * width), bf16)], [vm],
        [pltpu.VMEM((HB, HB * width, 128), f32)], big,
    )
    for step in range(WINDOW - 2, 0, -1):
        blocks, later, disp, vel, mass_b, coeff, _, now, out_a = call(
            functools.partial(main_rows, step), "main_rows",
            [blocks, later, disp, vel, mass_b, coeff, halo_a, now], [place], [sm],
            [edge_t], [vm], (), big,
        )
        now, later = later, now
        halo_a = lax.ppermute(out_a, RING, inner)
        dense, disp, vel, mass_b, _, later, out_b = call(
            edge_rows, "edge_rows", [dense, disp, vel, mass_b, halo_b, later], [], [],
            [edge_t], [vm],
        )
        halo_b = lax.ppermute(out_b, RING, outer)

    shape = jax.ShapeDtypeStruct((rows, width, lanes), f32)
    *_, disp, vel, _, _, disp_out, vel_out = call(
        main_last, "main_last", [blocks, later, disp, vel, coeff, halo_a], [place], [sm],
        [shape] * 2, [hbm] * 2, [dma((2, rows // HB - 1))], big,
    )
    return pl.pallas_call(
        edge_last,
        name="edge_last",
        out_shape=tuple(like(a) for a in (dense, disp, vel, halo_b)) + (shape,) * 2,
        in_specs=[vm] * 4 + [hbm] * 2,
        out_specs=(vm,) * 4 + (hbm,) * 2,
        input_output_aliases={i: i for i in range(6)},
        scratch_shapes=[dma((2, HB))],
        compiler_params=pltpu.CompilerParams(vmem_limit_bytes=VMEM_LIMIT),
        cost_estimate=small,
    )(dense, disp, vel, halo_b, disp_out, vel_out)[-2:]


def solution(mesh):
    placed = (
        P(("groups", "space", "rep"), None, "ckpt"),
        P(("groups", "space", "rep"), None, "ckpt"),
        P(("groups", "space", "rep"), None, None),
        P(("groups", "space", "rep"), None),
        P(("groups", "space", "rep"), None),
        P(("groups", "space", "rep"), None),
        P(None, ("groups", "space", "rep")),
        P(None, ("groups", "space", "rep"), "ckpt"),
    )
    return jax.shard_map(
        body,
        mesh=mesh,
        in_specs=placed,
        out_specs=(
            P(("groups", "space", "rep"), None, "ckpt"),
            P(("groups", "space", "rep"), None, "ckpt"),
        ),
        check_vma=False,
    )
```

```python
import functools
import jax
import jax.numpy as jnp
from jax import lax
from jax.experimental import pallas as pl
from jax.experimental.pallas import tpu as pltpu
from jax.sharding import PartitionSpec as P

HB = 4
WINDOW = 3
RING = ("space", "rep")
VMEM_LIMIT = 24 * 1024 * 1024


def ring_pairs(ring):
    inner = [(i, i ^ 1) for i in range(ring)]
    outer = [(i, (i + 1) % ring) for i in range(1, ring, 2)]
    outer = outer + [(b, a) for a, b in outer]
    return inner, outer


def windows_of(lanes):
    tiles = lanes // 128
    if tiles < 2:
        return [(0, lanes)]
    cut = 128 * ((tiles + 1) // 2)
    return [(0, cut), (cut, lanes - cut)]


def product(blocks, packed, place, r, window=None):
    slots = blocks.shape[2] // blocks.shape[1]
    at = slice(None) if window is None else pl.ds(*window)
    picked = jnp.concatenate([packed[place[k, r], :, at] for k in range(slots)], axis=0)
    return jnp.dot(blocks[r], picked, preferred_element_type=jnp.float32)


def tiled(column, lanes):
    return jnp.concatenate([column] * (lanes // 128), axis=1)


def spread(matrix, r, lanes):
    return jnp.broadcast_to(matrix[:, r : r + 1], (matrix.shape[0], lanes))


def each(count, one):
    def run(i, carry):
        one(i)
        return carry

    lax.fori_loop(0, count, run, 0, unroll=True)


def begin(copies):
    for c in copies:
        c.start()
    return copies


def end(copies):
    for c in copies:
        c.wait()


def head(vel0, inv_mass, *refs):
    *out_b, out_a, low, high, mass, sem = refs
    rows, _, lanes = vel0.shape
    end(
        begin(
            [
                pltpu.make_async_copy(inv_mass, mass, sem.at[0]),
                pltpu.make_async_copy(vel0.at[pl.ds(0, HB)], low, sem.at[1]),
                pltpu.make_async_copy(vel0.at[pl.ds(rows - HB, HB)], high, sem.at[2]),
            ]
        )
    )
    rep = lax.axis_index("rep")
    upright = mass[...].T
    for j in range(HB):
        p = spread(upright, j, lanes) * (0.5 * low[j].astype(jnp.float32))
        q = spread(upright, rows - HB + j, lanes) * (0.5 * high[j].astype(jnp.float32))
        b = jnp.where(rep == 0, p, q).astype(jnp.bfloat16)
        for ref, (at, size) in zip(out_b, windows_of(lanes)):
            ref[j] = b[:, at : at + size]
        out_a[j] = jnp.where(rep == 0, q, p).astype(jnp.bfloat16)


def load_all(total, blocks_in, vel0_in, disp0_in, inv_mass, stiff_in, contact_in, mine, cols_in, *refs):
    halo, blocks, now, disp, vel, mass_b, bent, turned, place_out = refs[:9]
    vel0, edges, cols, place, mass, stiff, contact, shard, sem = refs[9:]
    rows, _, lanes = vel0.shape
    rep = lax.axis_index("rep")
    a_start = (rows - HB) * (1 - rep)
    b_start = (rows - HB) * rep
    sides = (pl.ds(a_start, HB), pl.ds(b_start, HB))
    get_cols = begin([pltpu.make_async_copy(cols_in, cols, sem.at[0])])
    small = begin(
        [
            pltpu.make_async_copy(inv_mass, mass, sem.at[1]),
            pltpu.make_async_copy(stiff_in, stiff, sem.at[2]),
            pltpu.make_async_copy(contact_in, contact, sem.at[3]),
            pltpu.make_async_copy(mine, shard, sem.at[4]),
        ]
    )
    get_vel = begin([pltpu.make_async_copy(vel0_in, vel0, sem.at[5])])
    get_rest = begin(
        [
            pltpu.make_async_copy(blocks_in.at[at], blocks.at[at], sem.at[6 + n])
            for n, at in enumerate(sides)
        ]
        + [
            pltpu.make_async_copy(disp0_in.at[at], edges.at[n], sem.at[8 + n])
            for n, at in enumerate(sides)
        ]
    )
    now[rows + 2 * HB] = jnp.zeros(now.shape[1:], now.dtype)
    side = (rows + HB) * (1 - rep)
    for j in range(HB):
        now[side + j] = halo[j]
    end(get_cols)
    first = (lax.axis_index("space") * 2 + rep) * rows
    row = lax.broadcasted_iota(jnp.int32, cols.shape, 1)
    off = cols[...] - (first + row)
    off = jnp.where(off > HB, off - total, off)
    off = jnp.where(off < -HB, off + total, off)
    place_out[...] = row + HB + off
    get_place = begin([pltpu.make_async_copy(place_out, place, sem.at[0])])
    end(small)
    upright = mass[...].T
    for r in range(rows):
        mass_b[r] = spread(upright, r, 128)
    part = shard.shape[2]
    home = pl.ds(pl.multiple_of(lax.axis_index("ckpt") * part, 8), part)
    stiff3 = 3.0 * stiff[...].T
    for s in range(WINDOW):
        bent[s] = stiff3 * contact[s : s + 1, :].astype(jnp.float32)
        turned[s, home, :] = shard[s].T
    end(get_vel)
    for r in range(rows):
        v = vel0[r].astype(jnp.float32)
        vel[r] = v
        now[r + HB] = (tiled(mass_b[r], lanes) * (0.5 * v)).astype(jnp.bfloat16)
    end(get_place)
    end(get_rest)
    for j in range(HB):
        disp[b_start + j] = edges[1, j].astype(jnp.float32)

    def one(i):
        r = a_start + i
        disp[r] = edges[0, i].astype(jnp.float32) - product(blocks, now, place, r)

    each(HB, one)


def finish_row(r, image, later, disp, vel, mass_b, window=None):
    at = slice(None) if window is None else pl.ds(*window)
    d = disp[r, :, at] - image
    v = vel[r, :, at] + d
    disp[r, :, at] = d
    vel[r, :, at] = v
    if later is not None:
        p = (tiled(mass_b[r], image.shape[1]) * v).astype(jnp.bfloat16)
        later[r + HB, :, at] = p
        return p


def joint(step, r, now, coeff, window=None):
    at = slice(None) if window is None else pl.ds(*window)
    own = now[r + HB, :, at].astype(jnp.float32)
    return tiled(coeff[step, r], own.shape[1]) * own


def coefficients(pieces, *refs):
    now, disp, vel, mass_b, bent, turned, *others = refs[5 + pieces : 10 + 2 * pieces]
    later, coeff, out_a = refs[10 + 2 * pieces :]
    rows, _, lanes = disp.shape
    part = turned.shape[1] // pieces
    me = lax.axis_index("ckpt")
    last = WINDOW - 1
    for s in range(WINDOW):
        for j, piece in enumerate(others):
            source = lax.rem(me + 1 + j, pieces)
            turned[s, pl.ds(pl.multiple_of(source * part, 8), part), :] = piece[s].T
        turned[s] = bent[s] * turned[s] * turned[s]
    full = turned[last]
    for r in range(rows):
        coeff[last, r] = spread(full, r, 128)
    later[rows + 2 * HB] = jnp.zeros(later.shape[1:], later.dtype)
    start = (rows - HB) * (1 - lax.axis_index("rep"))

    def one(i):
        r = start + i
        out_a[i] = finish_row(r, joint(last, r, now, coeff), later, disp, vel, mass_b)

    each(HB, one)


def first_edge(window, *refs):
    place, blocks, now, disp, vel, mass_b, coeff, halo, later, out = refs[-10:]
    rows = disp.shape[0]
    rep = lax.axis_index("rep")
    at = pl.ds(*window)
    for j in range(HB):
        now[(rows + HB) * rep + j, :, at] = halo[j]
    start = (rows - HB) * rep

    def one(i):
        r = start + i
        image = product(blocks, now, place, r, window)
        image = image + joint(WINDOW - 1, r, now, coeff, window)
        out[i] = finish_row(r, image, later, disp, vel, mass_b, window)

    each(HB, one)


def first_interior(*refs):
    blocks_in, disp0_in, place = refs[8:11]
    blocks, now, later, disp, vel, mass_b, turned, coeff, dense, wide, disp0, sem = refs[11:]
    rows, width, lanes = disp.shape
    slots = blocks.shape[2] // width
    loads = []
    for g in range(1, rows // HB - 1):
        at = pl.ds(g * HB, HB)
        loads.append(
            begin(
                [
                    pltpu.make_async_copy(blocks_in.at[at], blocks.at[at], sem.at[0, g]),
                    pltpu.make_async_copy(disp0_in.at[at], disp0.at[at], sem.at[1, g]),
                ]
            )
        )
    for s in range(WINDOW - 1):
        full = turned[s]
        for r in range(rows):
            coeff[s, r] = spread(full, r, 128)
    rep = lax.axis_index("rep")
    wide[...] = jnp.zeros_like(wide)
    for i in range(HB):
        r = (rows - HB) * rep + i
        block = blocks[r].astype(jnp.float32)
        for k in range(slots):
            j = place[k, r] - (rows + HB) * rep
            inside = jnp.logical_and(j >= 0, j < HB)

            @pl.when(inside)
            def _():
                at = pl.ds(i * width, width)
                wide[j, at, pl.ds(0, width)] += block[:, k * width : (k + 1) * width]

    dense[...] = jnp.concatenate([wide[j, :, :width] for j in range(HB)], axis=1).astype(
        jnp.bfloat16
    )
    for g, load in enumerate(loads, 1):
        end(load)
        for r in range(g * HB, (g + 1) * HB):
            disp[r] = disp0[r].astype(jnp.float32)
            image = product(blocks, now, place, r) + joint(WINDOW - 1, r, now, coeff)
            finish_row(r, image, later, disp, vel, mass_b)


def near_part(step, i, blocks, now, place, coeff, disp):
    rows = disp.shape[0]
    rep = lax.axis_index("rep")
    r = (rows - HB) * rep + i
    low = (rows + HB) * rep
    slots = blocks.shape[2] // blocks.shape[1]
    picked = []
    for k in range(slots):
        p = place[k, r]
        inside = jnp.logical_and(p >= low, p < low + HB)
        picked.append(now[jnp.where(inside, rows + 2 * HB, p)])
    image = jnp.dot(
        blocks[r], jnp.concatenate(picked, axis=0), preferred_element_type=jnp.float32
    )
    disp[r] = disp[r] - (image + joint(step, r, now, coeff))


def main_rows(step, *refs):
    place, blocks, now, disp, vel, mass_b, coeff, halo, later, out = refs[-10:]
    rows = disp.shape[0]
    side = 1 - lax.axis_index("rep")
    for j in range(HB):
        now[(rows + HB) * side + j] = halo[j]
    start = HB * side

    def one(i):
        r = start + i
        image = product(blocks, now, place, r) + joint(step, r, now, coeff)
        finish_row(r, image, later, disp, vel, mass_b)

    each(rows - HB, one)
    for j in range(HB):
        out[j] = later[(rows - HB) * side + HB + j]
    each(HB, lambda i: near_part(step, i, blocks, now, place, coeff, disp))


def far_part(dense, halo):
    rows, width, lanes = halo.shape
    return jnp.dot(
        dense[...], halo[...].reshape(rows * width, lanes), preferred_element_type=jnp.float32
    )


def edge_rows(window, *refs):
    dense, disp, vel, mass_b, halo, later, out = refs[-7:]
    rows, width, _ = disp.shape
    image = far_part(dense, halo)
    start = (rows - HB) * lax.axis_index("rep")
    for i in range(HB):
        part = image[i * width : (i + 1) * width]
        out[i] = finish_row(start + i, part, later, disp, vel, mass_b, window)


def row_copies(disp, vel, disp_out, vel_out, sem, start, count, g, window):
    at = (pl.ds(start, count), slice(None), pl.ds(*window))
    return [
        pltpu.make_async_copy(disp.at[at], disp_out.at[at], sem.at[0, g]),
        pltpu.make_async_copy(vel.at[at], vel_out.at[at], sem.at[1, g]),
    ]


def main_last(*refs):
    place, blocks, now, disp, vel, coeff, halo, disp_out, vel_out, sem = refs[-10:]
    rows = disp.shape[0]
    side = 1 - lax.axis_index("rep")
    for j in range(HB):
        now[(rows + HB) * side + j] = halo[j]
    sent = []
    for g in range(rows // HB - 1):
        start = HB * side + g * HB

        def one(i):
            r = start + i
            image = product(blocks, now, place, r) + joint(0, r, now, coeff)
            finish_row(r, image, None, disp, vel, None)

        each(HB, one)
        copies = row_copies(disp, vel, disp_out, vel_out, sem, start, HB, g, (0, disp.shape[2]))
        sent += begin(copies)
    each(HB, lambda i: near_part(0, i, blocks, now, place, coeff, disp))
    end(sent)


def edge_last(window, *refs):
    dense, disp, vel, halo, disp_out, vel_out, sem = refs[-7:]
    rows, width, _ = disp.shape
    image = far_part(dense, halo)
    start = (rows - HB) * lax.axis_index("rep")
    sent = []
    for i in range(HB):
        part = image[i * width : (i + 1) * width]
        finish_row(start + i, part, None, disp, vel, None, window)
        sent += begin(row_copies(disp, vel, disp_out, vel_out, sem, start + i, 1, i, window))
    end(sent)


def body(adj_disp, adj_vel, tangent_blocks, block_cols, inv_mass, joint_stiff, contact, states):
    rows, width, lanes = adj_disp.shape
    ring = lax.axis_size(RING)
    total = rows * ring
    inner, outer = ring_pairs(ring)
    pieces = lax.axis_size("ckpt")
    f32, bf16 = jnp.float32, jnp.bfloat16
    vm = pl.BlockSpec(memory_space=pltpu.VMEM)
    sm = pl.BlockSpec(memory_space=pltpu.SMEM)
    hbm = pl.BlockSpec(memory_space=pltpu.HBM)
    like = lambda a: pltpu.VMEM(a.shape, a.dtype)
    edge_t = pltpu.VMEM((HB, width, lanes), bf16)
    ext = pltpu.VMEM((rows + 2 * HB + 1, width, lanes), bf16)
    full = pltpu.VMEM((rows, width, lanes), f32)
    table = pltpu.VMEM((rows, width), f32)
    upright = pltpu.VMEM((WINDOW, width, rows), f32)
    dma = pltpu.SemaphoreType.DMA
    light = pl.CostEstimate(flops=1000, bytes_accessed=1000, transcendentals=0)
    heavy = pl.CostEstimate(flops=4_000_000_000, bytes_accessed=1000, transcendentals=0)
    adj_disp, adj_vel, tangent_blocks, cols, inv_mass, joint_stiff, contact, mine = (
        pltpu.with_memory_space_constraint(a, pltpu.HBM)
        for a in (
            adj_disp, adj_vel, tangent_blocks, block_cols.T, inv_mass, joint_stiff, contact, states
        )
    )

    def call(kernel, name, held, given, specs, made, made_specs, scratch=(), cost=light):
        return pl.pallas_call(
            kernel,
            name=name,
            out_shape=tuple(like(a) for a in held) + tuple(made),
            in_specs=[vm] * len(held) + list(specs),
            out_specs=(vm,) * len(held) + tuple(made_specs),
            input_output_aliases={i: i for i in range(len(held))},
            scratch_shapes=list(scratch),
            compiler_params=pltpu.CompilerParams(vmem_limit_bytes=VMEM_LIMIT),
            cost_estimate=cost,
        )(*held, *given)

    windows = windows_of(lanes)
    edges_t = [pltpu.VMEM((HB, width, size), bf16) for _, size in windows]

    *out_b, out_a = call(
        head, "head", [], [adj_vel, inv_mass], [hbm] * 2,
        edges_t + [edge_t], [vm] * (len(windows) + 1), [edge_t, edge_t, table, dma((3,))],
    )
    states_late, out_a = lax.optimization_barrier((states, out_a))
    halo_a = lax.ppermute(out_a, RING, inner)
    halo_b = [lax.ppermute(a, RING, outer) for a in out_b]
    others = [
        lax.ppermute(states_late, "ckpt", [((i + j) % pieces, i) for i in range(pieces)])
        for j in range(1, pieces)
    ]

    _, blocks, now, disp, vel, mass_b, bent, turned, place = call(
        lambda *refs: load_all(total, *refs[1:9], refs[0], *refs[10:]), "load_all",
        [halo_a],
        [tangent_blocks, adj_vel, adj_disp, inv_mass, joint_stiff, contact, mine, cols], [hbm] * 8,
        [
            like(tangent_blocks), ext, full, full, pltpu.VMEM((rows, width, 128), f32),
            upright, upright, like(cols),
        ],
        [vm] * 8,
        [
            like(adj_vel), pltpu.VMEM((2, HB, width, lanes), bf16), like(cols),
            pltpu.SMEM(cols.shape, jnp.int32), table, table,
            pltpu.VMEM(contact.shape, jnp.int32), pltpu.VMEM(states.shape, f32), dma((10,)),
        ],
    )
    now, disp, vel, mass_b, _, turned, *_, later, coeff, out_a = call(
        functools.partial(coefficients, pieces), "coefficients",
        [now, disp, vel, mass_b, bent, turned] + others, [], [],
        [ext, pltpu.VMEM((WINDOW, rows, width, 128), f32), edge_t], [vm] * 3,
    )
    halo_a = lax.ppermute(out_a, RING, inner)
    for n, window in enumerate(windows):
        blocks, now, disp, vel, mass_b, coeff, _, later, out = call(
            functools.partial(first_edge, window), "first_edge",
            [blocks, now, disp, vel, mass_b, coeff, halo_b[n], later], [place], [sm],
            [edges_t[n]], [vm], (), heavy if n else light,
        )
        halo_b[n] = lax.ppermute(out, RING, outer)
    blocks, now, later, disp, vel, mass_b, _, coeff, dense = call(
        first_interior, "first_interior",
        [blocks, now, later, disp, vel, mass_b, turned, coeff],
        [tangent_blocks, adj_disp, place], [hbm, hbm, sm],
        [pltpu.VMEM((HB * width, HB * width), bf16)], [vm],
        [pltpu.VMEM((HB, HB * width, 128), f32), like(adj_disp), dma((2, rows // HB))],
    )
    for step in range(WINDOW - 2, 0, -1):
        blocks, later, disp, vel, mass_b, coeff, _, now, out_a = call(
            functools.partial(main_rows, step), "main_rows",
            [blocks, later, disp, vel, mass_b, coeff, halo_a, now], [place], [sm],
            [edge_t], [vm],
        )
        now, later = later, now
        halo_a = lax.ppermute(out_a, RING, inner)
        for n, window in enumerate(windows):
            dense, disp, vel, mass_b, _, later, out = call(
                functools.partial(edge_rows, window), "edge_rows",
                [dense, disp, vel, mass_b, halo_b[n], later], [], [], [edges_t[n]], [vm],
                (), heavy if n else light,
            )
            halo_b[n] = lax.ppermute(out, RING, outer)

    shape = jax.ShapeDtypeStruct((rows, width, lanes), f32)
    *_, disp, vel, _, _, disp_out, vel_out = call(
        main_last, "main_last", [blocks, later, disp, vel, coeff, halo_a], [place], [sm],
        [shape] * 2, [hbm] * 2, [dma((2, rows // HB - 1))],
    )
    for n, window in enumerate(windows):
        dense, disp, vel, _, disp_out, vel_out = pl.pallas_call(
            functools.partial(edge_last, window),
            name="edge_last",
            out_shape=tuple(like(a) for a in (dense, disp, vel, halo_b[n])) + (shape,) * 2,
            in_specs=[vm] * 4 + [hbm] * 2,
            out_specs=(vm,) * 4 + (hbm,) * 2,
            input_output_aliases={i: i for i in range(6)},
            scratch_shapes=[dma((2, HB))],
            compiler_params=pltpu.CompilerParams(vmem_limit_bytes=VMEM_LIMIT),
            cost_estimate=light,
        )(dense, disp, vel, halo_b[n], disp_out, vel_out)
    return disp_out, vel_out


def solution(mesh):
    placed = (
        P(("groups", "space", "rep"), None, "ckpt"),
        P(("groups", "space", "rep"), None, "ckpt"),
        P(("groups", "space", "rep"), None, None),
        P(("groups", "space", "rep"), None),
        P(("groups", "space", "rep"), None),
        P(("groups", "space", "rep"), None),
        P(None, ("groups", "space", "rep")),
        P(None, ("groups", "space", "rep"), "ckpt"),
    )
    return jax.shard_map(
        body,
        mesh=mesh,
        in_specs=placed,
        out_specs=(
            P(("groups", "space", "rep"), None, "ckpt"),
            P(("groups", "space", "rep"), None, "ckpt"),
        ),
        check_vma=False,
    )
```

```python
import functools
import jax
import jax.numpy as jnp
from jax import lax
from jax.experimental import pallas as pl
from jax.experimental.pallas import tpu as pltpu
from jax.sharding import PartitionSpec as P

HB = 4
WINDOW = 3
RING = ("space", "rep")
VMEM_LIMIT = 24 * 1024 * 1024


def ring_pairs(ring):
    inner = [(i, i ^ 1) for i in range(ring)]
    outer = [(i, (i + 1) % ring) for i in range(1, ring, 2)]
    outer = outer + [(b, a) for a, b in outer]
    return inner, outer


def windows_of(lanes):
    tiles = lanes // 128
    if tiles < 2:
        return [(0, lanes)]
    cut = 128 * ((tiles + 1) // 2)
    return [(0, cut), (cut, lanes - cut)]


def product(blocks, packed, place, r, window=None):
    slots = blocks.shape[2] // blocks.shape[1]
    at = slice(None) if window is None else pl.ds(*window)
    picked = jnp.concatenate([packed[place[k, r], :, at] for k in range(slots)], axis=0)
    return jnp.dot(blocks[r], picked, preferred_element_type=jnp.float32)


def tiled(column, lanes):
    return jnp.concatenate([column] * (lanes // 128), axis=1)


def spread(matrix, r, lanes):
    return jnp.broadcast_to(matrix[:, r : r + 1], (matrix.shape[0], lanes))


def each(count, one):
    def run(i, carry):
        one(i)
        return carry

    lax.fori_loop(0, count, run, 0, unroll=True)


def begin(copies):
    for c in copies:
        c.start()
    return copies


def end(copies):
    for c in copies:
        c.wait()


def head(vel0, inv_mass, *refs):
    out_b, out_a, low, high, mass, sem = refs
    rows, _, lanes = vel0.shape
    end(
        begin(
            [
                pltpu.make_async_copy(inv_mass, mass, sem.at[0]),
                pltpu.make_async_copy(vel0.at[pl.ds(0, HB)], low, sem.at[1]),
                pltpu.make_async_copy(vel0.at[pl.ds(rows - HB, HB)], high, sem.at[2]),
            ]
        )
    )
    rep = lax.axis_index("rep")
    upright = mass[...].T
    for j in range(HB):
        p = spread(upright, j, lanes) * (0.5 * low[j].astype(jnp.float32))
        q = spread(upright, rows - HB + j, lanes) * (0.5 * high[j].astype(jnp.float32))
        out_b[j] = jnp.where(rep == 0, p, q).astype(jnp.bfloat16)
        out_a[j] = jnp.where(rep == 0, q, p).astype(jnp.bfloat16)


def load_all(total, blocks_in, vel0_in, disp0_in, inv_mass, stiff_in, contact_in, mine, cols_in, *refs):
    halo, blocks, disp0, now, disp, vel, mass_b, bent, turned, place_out = refs[:10]
    vel0, cols, place, mass, stiff, contact, shard, sem = refs[10:]
    rows, _, lanes = vel0.shape
    rep = lax.axis_index("rep")
    a_start = (rows - HB) * (1 - rep)
    b_start = (rows - HB) * rep
    sides = (pl.ds(a_start, HB), pl.ds(b_start, HB), pl.ds(HB, rows - 2 * HB))
    get_cols = begin([pltpu.make_async_copy(cols_in, cols, sem.at[0])])
    small = begin(
        [
            pltpu.make_async_copy(inv_mass, mass, sem.at[1]),
            pltpu.make_async_copy(stiff_in, stiff, sem.at[2]),
            pltpu.make_async_copy(contact_in, contact, sem.at[3]),
            pltpu.make_async_copy(mine, shard, sem.at[4]),
        ]
    )
    get_vel = begin([pltpu.make_async_copy(vel0_in, vel0, sem.at[5])])
    get_rest = [
        begin(
            [
                pltpu.make_async_copy(blocks_in.at[at], blocks.at[at], sem.at[6 + 2 * n]),
                pltpu.make_async_copy(disp0_in.at[at], disp0.at[at], sem.at[7 + 2 * n]),
            ]
        )
        for n, at in enumerate(sides)
    ]
    now[rows + 2 * HB] = jnp.zeros(now.shape[1:], now.dtype)
    side = (rows + HB) * (1 - rep)
    for j in range(HB):
        now[side + j] = halo[j]
    end(get_cols)
    first = (lax.axis_index("space") * 2 + rep) * rows
    row = lax.broadcasted_iota(jnp.int32, cols.shape, 1)
    off = cols[...] - (first + row)
    off = jnp.where(off > HB, off - total, off)
    off = jnp.where(off < -HB, off + total, off)
    place_out[...] = row + HB + off
    get_place = begin([pltpu.make_async_copy(place_out, place, sem.at[0])])
    end(small)
    upright = mass[...].T
    for r in range(rows):
        mass_b[r] = spread(upright, r, 128)
    part = shard.shape[2]
    home = pl.ds(pl.multiple_of(lax.axis_index("ckpt") * part, 8), part)
    stiff3 = 3.0 * stiff[...].T
    for s in range(WINDOW):
        bent[s] = stiff3 * contact[s : s + 1, :].astype(jnp.float32)
        turned[s, home, :] = shard[s].T
    end(get_vel)
    for r in range(rows):
        v = vel0[r].astype(jnp.float32)
        vel[r] = v
        now[r + HB] = (tiled(mass_b[r], lanes) * (0.5 * v)).astype(jnp.bfloat16)
    end(get_place)
    end(get_rest[0])

    def one(i):
        r = a_start + i
        disp[r] = disp0[r].astype(jnp.float32) - product(blocks, now, place, r)

    each(HB, one)
    end(get_rest[1])
    for j in range(HB):
        disp[b_start + j] = disp0[b_start + j].astype(jnp.float32)
    end(get_rest[2])


def finish_row(r, image, later, disp, vel, mass_b, window=None):
    at = slice(None) if window is None else pl.ds(*window)
    d = disp[r, :, at] - image
    v = vel[r, :, at] + d
    disp[r, :, at] = d
    vel[r, :, at] = v
    if later is not None:
        p = (tiled(mass_b[r], image.shape[1]) * v).astype(jnp.bfloat16)
        later[r + HB, :, at] = p
        return p


def joint(r, now, coeff):
    return tiled(coeff[r], now.shape[2]) * now[r + HB].astype(jnp.float32)


def spread_rows(matrix, out):
    for r in range(out.shape[0]):
        out[r] = spread(matrix, r, 128)


def coefficients(pieces, *refs):
    now, disp, vel, mass_b, bent, turned, *others = refs[5 + pieces : 10 + 2 * pieces]
    later, coeff, out_a = refs[10 + 2 * pieces :]
    rows, _, lanes = disp.shape
    part = turned.shape[1] // pieces
    me = lax.axis_index("ckpt")
    last = WINDOW - 1
    for s in range(WINDOW):
        for j, piece in enumerate(others):
            source = lax.rem(me + 1 + j, pieces)
            turned[s, pl.ds(pl.multiple_of(source * part, 8), part), :] = piece[s].T
        turned[s] = bent[s] * turned[s] * turned[s]
    spread_rows(turned[last], coeff)
    later[rows + 2 * HB] = jnp.zeros(later.shape[1:], later.dtype)
    start = (rows - HB) * (1 - lax.axis_index("rep"))

    def one(i):
        r = start + i
        out_a[i] = finish_row(r, joint(r, now, coeff), later, disp, vel, mass_b)

    each(HB, one)


def first_interior(*refs):
    place, blocks, disp0, now, later, disp, vel, mass_b, coeff, dense = refs[-10:]
    rows, width, _ = disp.shape
    slots = blocks.shape[2] // width
    side = lax.axis_index("rep")
    shape = (width, HB * width)
    ahead = lax.broadcasted_iota(jnp.int32, shape, 1) - lax.broadcasted_iota(jnp.int32, shape, 0)
    for i in range(HB):
        r = (rows - HB) * side + i
        chosen = []
        for k in range(slots):
            j = place[k, r] - (rows + HB) * side
            inside = jnp.logical_and(j >= 0, j < HB)
            at = jnp.where(inside, j * width, -width)
            chosen.append(jnp.where(ahead == at, 1.0, 0.0).astype(jnp.bfloat16))
        picked = jnp.dot(
            blocks[r], jnp.concatenate(chosen, axis=0), preferred_element_type=jnp.float32
        )
        dense[pl.ds(i * width, width), :] = picked.astype(jnp.bfloat16)

    def one(i):
        r = HB + i
        disp[r] = disp0[r].astype(jnp.float32)
        image = product(blocks, now, place, r) + joint(r, now, coeff)
        finish_row(r, image, later, disp, vel, mass_b)

    each(rows - 2 * HB, one)
    each(HB, lambda i: near_part(i, blocks, now, place, coeff, disp))


def near_part(i, blocks, now, place, coeff, disp):
    rows = disp.shape[0]
    rep = lax.axis_index("rep")
    r = (rows - HB) * rep + i
    low = (rows + HB) * rep
    slots = blocks.shape[2] // blocks.shape[1]
    picked = []
    for k in range(slots):
        p = place[k, r]
        inside = jnp.logical_and(p >= low, p < low + HB)
        picked.append(now[jnp.where(inside, rows + 2 * HB, p)])
    image = jnp.dot(
        blocks[r], jnp.concatenate(picked, axis=0), preferred_element_type=jnp.float32
    )
    disp[r] = disp[r] - (image + joint(r, now, coeff))


def main_rows(step, *refs):
    place, blocks, now, disp, vel, mass_b, turned, coeff, halo, later, out = refs[-11:]
    rows = disp.shape[0]
    spread_rows(turned[step], coeff)
    side = 1 - lax.axis_index("rep")
    for j in range(HB):
        now[(rows + HB) * side + j] = halo[j]
    start = HB * side

    def one(i):
        r = start + i
        image = product(blocks, now, place, r) + joint(r, now, coeff)
        finish_row(r, image, later, disp, vel, mass_b)

    each(rows - HB, one)
    for j in range(HB):
        out[j] = later[(rows - HB) * side + HB + j]
    each(HB, lambda i: near_part(i, blocks, now, place, coeff, disp))


def far_part(dense, halo, window):
    rows, width, lanes = halo.shape
    start, size = window
    start = start if lanes > size else 0
    seen = halo[:, :, start : start + size].reshape(rows * width, size)
    return jnp.dot(dense[...], seen, preferred_element_type=jnp.float32)


def edge_rows(window, *refs):
    dense, disp, vel, mass_b, halo, later, out = refs[-7:]
    rows, width, _ = disp.shape
    image = far_part(dense, halo, window)
    start = (rows - HB) * lax.axis_index("rep")
    for i in range(HB):
        part = image[i * width : (i + 1) * width]
        out[i] = finish_row(start + i, part, later, disp, vel, mass_b, window)


def row_copies(disp, vel, disp_out, vel_out, sem, start, count, g, window):
    at = (pl.ds(start, count), slice(None), pl.ds(*window))
    return [
        pltpu.make_async_copy(disp.at[at], disp_out.at[at], sem.at[0, g]),
        pltpu.make_async_copy(vel.at[at], vel_out.at[at], sem.at[1, g]),
    ]


def main_last(*refs):
    place, blocks, now, disp, vel, turned, coeff, halo, disp_out, vel_out, sem = refs[-11:]
    rows = disp.shape[0]
    spread_rows(turned[0], coeff)
    side = 1 - lax.axis_index("rep")
    for j in range(HB):
        now[(rows + HB) * side + j] = halo[j]
    sent = []
    for g in range(rows // HB - 1):
        start = HB * side + g * HB

        def one(i):
            r = start + i
            image = product(blocks, now, place, r) + joint(r, now, coeff)
            finish_row(r, image, None, disp, vel, None)

        each(HB, one)
        copies = row_copies(disp, vel, disp_out, vel_out, sem, start, HB, g, (0, disp.shape[2]))
        sent += begin(copies)
    each(HB, lambda i: near_part(i, blocks, now, place, coeff, disp))
    end(sent)


def edge_last(window, *refs):
    dense, disp, vel, halo, disp_out, vel_out, sem = refs[-7:]
    rows, width, _ = disp.shape
    image = far_part(dense, halo, window)
    start = (rows - HB) * lax.axis_index("rep")
    sent = []
    for i in range(HB):
        part = image[i * width : (i + 1) * width]
        finish_row(start + i, part, None, disp, vel, None, window)
        sent += begin(row_copies(disp, vel, disp_out, vel_out, sem, start + i, 1, i, window))
    end(sent)


def body(adj_disp, adj_vel, tangent_blocks, block_cols, inv_mass, joint_stiff, contact, states):
    rows, width, lanes = adj_disp.shape
    ring = lax.axis_size(RING)
    total = rows * ring
    inner, outer = ring_pairs(ring)
    pieces = lax.axis_size("ckpt")
    f32, bf16 = jnp.float32, jnp.bfloat16
    vm = pl.BlockSpec(memory_space=pltpu.VMEM)
    sm = pl.BlockSpec(memory_space=pltpu.SMEM)
    hbm = pl.BlockSpec(memory_space=pltpu.HBM)
    like = lambda a: pltpu.VMEM(a.shape, a.dtype)
    edge_t = pltpu.VMEM((HB, width, lanes), bf16)
    ext = pltpu.VMEM((rows + 2 * HB + 1, width, lanes), bf16)
    full = pltpu.VMEM((rows, width, lanes), f32)
    table = pltpu.VMEM((rows, width), f32)
    upright = pltpu.VMEM((WINDOW, width, rows), f32)
    dma = pltpu.SemaphoreType.DMA
    light = pl.CostEstimate(flops=1000, bytes_accessed=1000, transcendentals=0)
    heavy = pl.CostEstimate(flops=4_000_000_000, bytes_accessed=1000, transcendentals=0)
    adj_disp, adj_vel, tangent_blocks, cols, inv_mass, joint_stiff, contact, mine = (
        pltpu.with_memory_space_constraint(a, pltpu.HBM)
        for a in (
            adj_disp, adj_vel, tangent_blocks, block_cols.T, inv_mass, joint_stiff, contact, states
        )
    )

    def call(kernel, name, held, given, specs, made, made_specs, scratch=(), cost=light):
        return pl.pallas_call(
            kernel,
            name=name,
            out_shape=tuple(like(a) for a in held) + tuple(made),
            in_specs=[vm] * len(held) + list(specs),
            out_specs=(vm,) * len(held) + tuple(made_specs),
            input_output_aliases={i: i for i in range(len(held))},
            scratch_shapes=list(scratch),
            compiler_params=pltpu.CompilerParams(vmem_limit_bytes=VMEM_LIMIT),
            cost_estimate=cost,
        )(*held, *given)

    windows = windows_of(lanes)
    edges_t = [pltpu.VMEM((HB, width, size), bf16) for _, size in windows]

    out_b, out_a = call(
        head, "head", [], [adj_vel, inv_mass], [hbm] * 2, [edge_t] * 2, [vm] * 2,
        [edge_t, edge_t, table, dma((3,))],
    )
    states_late, out_a = lax.optimization_barrier((states, out_a))
    halo_a = lax.ppermute(out_a, RING, inner)
    whole_b = lax.ppermute(out_b, RING, outer)
    halo_b = [whole_b] * len(windows)
    others = [
        lax.ppermute(states_late, "ckpt", [((i + j) % pieces, i) for i in range(pieces)])
        for j in range(1, pieces)
    ]

    _, blocks, disp0, now, disp, vel, mass_b, bent, turned, place = call(
        lambda *refs: load_all(total, *refs[1:9], refs[0], *refs[10:]), "load_all",
        [halo_a],
        [tangent_blocks, adj_vel, adj_disp, inv_mass, joint_stiff, contact, mine, cols], [hbm] * 8,
        [
            like(tangent_blocks), like(adj_disp), ext, full, full,
            pltpu.VMEM((rows, width, 128), f32), upright, upright, like(cols),
        ],
        [vm] * 9,
        [
            like(adj_vel), like(cols), pltpu.SMEM(cols.shape, jnp.int32), table, table,
            pltpu.VMEM(contact.shape, jnp.int32), pltpu.VMEM(states.shape, f32), dma((12,)),
        ],
    )
    now, disp, vel, mass_b, _, turned, *_, later, coeff, out_a = call(
        functools.partial(coefficients, pieces), "coefficients",
        [now, disp, vel, mass_b, bent, turned] + others, [], [],
        [ext, like(mass_b), edge_t], [vm] * 3,
    )
    halo_a = lax.ppermute(out_a, RING, inner)
    blocks, _, now, later, disp, vel, mass_b, coeff, dense = call(
        first_interior, "first_interior",
        [blocks, disp0, now, later, disp, vel, mass_b, coeff], [place], [sm],
        [pltpu.VMEM((HB * width, HB * width), bf16)], [vm],
    )
    for step in range(WINDOW - 1, 0, -1):
        if step < WINDOW - 1:
            blocks, later, disp, vel, mass_b, turned, coeff, _, now, out_a = call(
                functools.partial(main_rows, step), "main_rows",
                [blocks, later, disp, vel, mass_b, turned, coeff, halo_a, now], [place], [sm],
                [edge_t], [vm],
            )
            now, later = later, now
            halo_a = lax.ppermute(out_a, RING, inner)
        sent = []
        for n, window in enumerate(windows):
            dense, disp, vel, mass_b, halo, later, out = call(
                functools.partial(edge_rows, window), "edge_rows",
                [dense, disp, vel, mass_b, halo_b[n], later], [], [], [edges_t[n]], [vm],
                (), heavy if n else light,
            )
            sent.append(lax.ppermute(out, RING, outer))
            if step == WINDOW - 1:
                halo_b = [halo] * len(windows)
        halo_b = sent

    shape = jax.ShapeDtypeStruct((rows, width, lanes), f32)
    *_, disp, vel, _, _, _, disp_out, vel_out = call(
        main_last, "main_last", [blocks, later, disp, vel, turned, coeff, halo_a], [place], [sm],
        [shape] * 2, [hbm] * 2, [dma((2, rows // HB - 1))],
    )
    for n, window in enumerate(windows):
        dense, disp, vel, _, disp_out, vel_out = pl.pallas_call(
            functools.partial(edge_last, window),
            name="edge_last",
            out_shape=tuple(like(a) for a in (dense, disp, vel, halo_b[n])) + (shape,) * 2,
            in_specs=[vm] * 4 + [hbm] * 2,
            out_specs=(vm,) * 4 + (hbm,) * 2,
            input_output_aliases={i: i for i in range(6)},
            scratch_shapes=[dma((2, HB))],
            compiler_params=pltpu.CompilerParams(vmem_limit_bytes=VMEM_LIMIT),
            cost_estimate=light,
        )(dense, disp, vel, halo_b[n], disp_out, vel_out)
    return disp_out, vel_out


def solution(mesh):
    placed = (
        P(("groups", "space", "rep"), None, "ckpt"),
        P(("groups", "space", "rep"), None, "ckpt"),
        P(("groups", "space", "rep"), None, None),
        P(("groups", "space", "rep"), None),
        P(("groups", "space", "rep"), None),
        P(("groups", "space", "rep"), None),
        P(None, ("groups", "space", "rep")),
        P(None, ("groups", "space", "rep"), "ckpt"),
    )
    return jax.shard_map(
        body,
        mesh=mesh,
        in_specs=placed,
        out_specs=(
            P(("groups", "space", "rep"), None, "ckpt"),
            P(("groups", "space", "rep"), None, "ckpt"),
        ),
        check_vma=False,
    )
```

```python
import functools
import jax
import jax.numpy as jnp
from jax import lax
from jax.experimental import pallas as pl
from jax.experimental.pallas import tpu as pltpu
from jax.sharding import PartitionSpec as P

HB = 4
WINDOW = 3
RING = ("space", "rep")
VMEM_LIMIT = 24 * 1024 * 1024
LATE = 8


def ring_pairs(ring):
    inner = [(i, i ^ 1) for i in range(ring)]
    outer = [(i, (i + 1) % ring) for i in range(1, ring, 2)]
    outer = outer + [(b, a) for a, b in outer]
    return inner, outer


def windows_of(lanes):
    tiles = lanes // 128
    if tiles < 2:
        return [(0, lanes)]
    cut = 128 * ((tiles + 1) // 2)
    return [(0, cut), (cut, lanes - cut)]


def product(blocks, packed, place, r, window=None):
    slots = blocks.shape[2] // blocks.shape[1]
    at = slice(None) if window is None else pl.ds(*window)
    picked = jnp.concatenate([packed[place[k, r], :, at] for k in range(slots)], axis=0)
    return jnp.dot(blocks[r], picked, preferred_element_type=jnp.float32)


def tiled(column, lanes):
    return jnp.concatenate([column] * (lanes // 128), axis=1)


def spread(matrix, r, lanes):
    return jnp.broadcast_to(matrix[:, r : r + 1], (matrix.shape[0], lanes))


def each(count, one):
    def run(i, carry):
        one(i)
        return carry

    lax.fori_loop(0, count, run, 0, unroll=True)


def begin(copies):
    for c in copies:
        c.start()
    return copies


def end(copies):
    for c in copies:
        c.wait()


def head(vel0, inv_mass, *refs):
    out_b, *out_a, low, high, mass, sem = refs
    rows, _, lanes = vel0.shape
    end(
        begin(
            [
                pltpu.make_async_copy(inv_mass, mass, sem.at[0]),
                pltpu.make_async_copy(vel0.at[pl.ds(0, HB)], low, sem.at[1]),
                pltpu.make_async_copy(vel0.at[pl.ds(rows - HB, HB)], high, sem.at[2]),
            ]
        )
    )
    rep = lax.axis_index("rep")
    upright = mass[...].T
    for j in range(HB):
        p = spread(upright, j, lanes) * (0.5 * low[j].astype(jnp.float32))
        q = spread(upright, rows - HB + j, lanes) * (0.5 * high[j].astype(jnp.float32))
        out_b[j] = jnp.where(rep == 0, p, q).astype(jnp.bfloat16)
        a = jnp.where(rep == 0, q, p).astype(jnp.bfloat16)
        for ref, (at, size) in zip(out_a, windows_of(lanes)):
            ref[j] = a[:, at : at + size]


def load_all(total, blocks_in, vel0_in, disp0_in, inv_mass, stiff_in, contact_in, mine, cols_in, *refs):
    blocks, disp0, now, disp, vel, mass_b, bent, turned, place_out, dense = refs[:10]
    vel0, cols, place, mass, stiff, contact, shard, sem = refs[10:]
    rows, width, lanes = vel0.shape
    rep = lax.axis_index("rep")
    b_start = (rows - HB) * rep
    sides = (pl.ds(b_start, HB), pl.ds(HB, rows - 2 * HB), pl.ds((rows - HB) * (1 - rep), HB))
    get_cols = begin([pltpu.make_async_copy(cols_in, cols, sem.at[0])])
    small = begin(
        [
            pltpu.make_async_copy(inv_mass, mass, sem.at[1]),
            pltpu.make_async_copy(stiff_in, stiff, sem.at[2]),
            pltpu.make_async_copy(contact_in, contact, sem.at[3]),
            pltpu.make_async_copy(mine, shard, sem.at[4]),
        ]
    )
    get_vel = begin([pltpu.make_async_copy(vel0_in, vel0, sem.at[5])])
    get_rest = [
        begin(
            [
                pltpu.make_async_copy(blocks_in.at[at], blocks.at[at], sem.at[6 + 2 * n]),
                pltpu.make_async_copy(disp0_in.at[at], disp0.at[at], sem.at[7 + 2 * n]),
            ]
        )
        for n, at in enumerate(sides)
    ]
    now[rows + 2 * HB] = jnp.zeros(now.shape[1:], now.dtype)
    end(get_cols)
    first = (lax.axis_index("space") * 2 + rep) * rows
    row = lax.broadcasted_iota(jnp.int32, cols.shape, 1)
    off = cols[...] - (first + row)
    off = jnp.where(off > HB, off - total, off)
    off = jnp.where(off < -HB, off + total, off)
    place_out[...] = row + HB + off
    get_place = begin([pltpu.make_async_copy(place_out, place, sem.at[0])])
    end(small)
    upright = mass[...].T
    for r in range(rows):
        mass_b[r] = spread(upright, r, 128)
    part = shard.shape[2]
    home = pl.ds(pl.multiple_of(lax.axis_index("ckpt") * part, 8), part)
    stiff3 = 3.0 * stiff[...].T
    for s in range(WINDOW):
        bent[s] = stiff3 * contact[s : s + 1, :].astype(jnp.float32)
        turned[s, home, :] = shard[s].T
    end(get_vel)
    for r in range(rows):
        v = vel0[r].astype(jnp.float32)
        vel[r] = v
        now[r + HB] = (tiled(mass_b[r], lanes) * (0.5 * v)).astype(jnp.bfloat16)
    end(get_place)
    end(get_rest[0])
    slots = blocks.shape[2] // width
    shape = (width, HB * width)
    ahead = lax.broadcasted_iota(jnp.int32, shape, 1) - lax.broadcasted_iota(jnp.int32, shape, 0)
    for i in range(HB):
        r = b_start + i
        chosen = []
        for k in range(slots):
            j = place[k, r] - (rows + HB) * rep
            inside = jnp.logical_and(j >= 0, j < HB)
            at = jnp.where(inside, j * width, -width)
            chosen.append(jnp.where(ahead == at, 1.0, 0.0).astype(jnp.bfloat16))
        picked = jnp.dot(
            blocks[r], jnp.concatenate(chosen, axis=0), preferred_element_type=jnp.float32
        )
        dense[pl.ds(i * width, width), :] = picked.astype(jnp.bfloat16)
    for i in range(HB):
        r = b_start + i
        disp[r] = disp0[r].astype(jnp.float32) - near_product(i, blocks, now, place)
    end(get_rest[1])
    end(get_rest[2])


def finish_row(r, image, later, disp, vel, mass_b, window=None):
    at = slice(None) if window is None else pl.ds(*window)
    d = disp[r, :, at] - image
    v = vel[r, :, at] + d
    disp[r, :, at] = d
    vel[r, :, at] = v
    if later is not None:
        p = (tiled(mass_b[r], image.shape[1]) * v).astype(jnp.bfloat16)
        later[r + HB, :, at] = p
        return p


def joint(r, now, coeff):
    return tiled(coeff[r], now.shape[2]) * now[r + HB].astype(jnp.float32)


def spread_rows(matrix, out):
    for r in range(out.shape[0]):
        out[r] = spread(matrix, r, 128)


def near_product(i, blocks, now, place):
    rows = blocks.shape[0]
    rep = lax.axis_index("rep")
    r = (rows - HB) * rep + i
    low = (rows + HB) * rep
    slots = blocks.shape[2] // blocks.shape[1]
    picked = []
    for k in range(slots):
        p = place[k, r]
        inside = jnp.logical_and(p >= low, p < low + HB)
        picked.append(now[jnp.where(inside, rows + 2 * HB, p)])
    return jnp.dot(
        blocks[r], jnp.concatenate(picked, axis=0), preferred_element_type=jnp.float32
    )


def near_part(i, blocks, now, place, coeff, disp):
    rows = disp.shape[0]
    r = (rows - HB) * lax.axis_index("rep") + i
    disp[r] = disp[r] - (near_product(i, blocks, now, place) + joint(r, now, coeff))


def full_rows(start, count, blocks, now, later, disp_old, disp, vel, mass_b, coeff, place, out=None):
    def one(i):
        r = start + i
        if disp_old is not None:
            disp[r] = disp_old[r].astype(jnp.float32)
        image = product(blocks, now, place, r) + joint(r, now, coeff)
        p = finish_row(r, image, later, disp, vel, mass_b)
        if out is not None:
            out[i] = p

    each(count, one)


def first_step(pieces, *refs):
    held = (len(refs) - 4) // 2
    place = refs[held]
    blocks, disp0, now, disp, vel, mass_b, bent, turned, *halo = refs[held + 1 : -3 - (pieces - 1)]
    others = refs[-3 - (pieces - 1) : -3]
    later, coeff, out_a = refs[-3:]
    rows = disp.shape[0]
    part = turned.shape[1] // pieces
    me = lax.axis_index("ckpt")
    rep = lax.axis_index("rep")
    for s in range(WINDOW):
        for j, piece in enumerate(others):
            source = lax.rem(me + 1 + j, pieces)
            turned[s, pl.ds(pl.multiple_of(source * part, 8), part), :] = piece[s].T
        turned[s] = bent[s] * turned[s] * turned[s]
    spread_rows(turned[WINDOW - 1], coeff)
    later[rows + 2 * HB] = jnp.zeros(later.shape[1:], later.dtype)
    for j in range(HB):
        for ref, window in zip(halo, windows_of(now.shape[2])):
            now[(rows + HB) * (1 - rep) + j, :, pl.ds(*window)] = ref[j]
    state = (blocks, now, later, disp0, disp, vel, mass_b, coeff, place)
    full_rows((rows - HB) * (1 - rep), HB, *state, out_a)
    full_rows(HB, rows - 2 * HB - min(LATE, rows - 2 * HB), *state)
    for i in range(HB):
        r = (rows - HB) * rep + i
        disp[r] = disp[r] - joint(r, now, coeff)


def main_rows(step, *refs):
    place, blocks, now, disp, vel, mass_b, turned, coeff, halo, later, *disp0, out = refs[
        -11 - (step == WINDOW - 2) :
    ]
    rows = disp.shape[0]
    late = min(LATE, rows - 2 * HB)
    if disp0:
        first = (later, now, disp0[0], disp, vel, mass_b, coeff, place)
        full_rows(rows - HB - late, late, blocks, *first)
    spread_rows(turned[step], coeff)
    side = 1 - lax.axis_index("rep")
    for j in range(HB):
        now[(rows + HB) * side + j] = halo[j]
    state = (blocks, now, later, None, disp, vel, mass_b, coeff, place)
    full_rows(HB * side, rows - HB, *state)
    for j in range(HB):
        out[j] = later[(rows - HB) * side + HB + j]
    each(HB, lambda i: near_part(i, blocks, now, place, coeff, disp))


def far_part(dense, halo, window):
    rows, width, lanes = halo.shape
    start, size = window
    start = start if lanes > size else 0
    seen = halo[:, :, start : start + size].reshape(rows * width, size)
    return jnp.dot(dense[...], seen, preferred_element_type=jnp.float32)


def edge_rows(window, *refs):
    dense, disp, vel, mass_b, halo, later, out = refs[-7:]
    rows, width, _ = disp.shape
    image = far_part(dense, halo, window)
    start = (rows - HB) * lax.axis_index("rep")
    for i in range(HB):
        part = image[i * width : (i + 1) * width]
        out[i] = finish_row(start + i, part, later, disp, vel, mass_b, window)


def row_copies(disp, vel, disp_out, vel_out, sem, start, count, g, window):
    at = (pl.ds(start, count), slice(None), pl.ds(*window))
    return [
        pltpu.make_async_copy(disp.at[at], disp_out.at[at], sem.at[0, g]),
        pltpu.make_async_copy(vel.at[at], vel_out.at[at], sem.at[1, g]),
    ]


def main_last(*refs):
    place, blocks, now, disp, vel, turned, coeff, halo, disp_out, vel_out, sem = refs[-11:]
    rows = disp.shape[0]
    spread_rows(turned[0], coeff)
    side = 1 - lax.axis_index("rep")
    for j in range(HB):
        now[(rows + HB) * side + j] = halo[j]
    sent = []
    for g in range(rows // HB - 1):
        start = HB * side + g * HB

        def one(i):
            r = start + i
            image = product(blocks, now, place, r) + joint(r, now, coeff)
            finish_row(r, image, None, disp, vel, None)

        each(HB, one)
        copies = row_copies(disp, vel, disp_out, vel_out, sem, start, HB, g, (0, disp.shape[2]))
        sent += begin(copies)
    each(HB, lambda i: near_part(i, blocks, now, place, coeff, disp))
    end(sent)


def edge_compute(window, *refs):
    dense, disp, vel, halo = refs[-4:]
    rows, width, _ = disp.shape
    image = far_part(dense, halo, window)
    start = (rows - HB) * lax.axis_index("rep")
    for i in range(HB):
        part = image[i * width : (i + 1) * width]
        finish_row(start + i, part, None, disp, vel, None, window)


def edge_last(window, *refs):
    dense, disp, vel, halo, disp_out, vel_out, sem = refs[-7:]
    rows, width, _ = disp.shape
    start = (rows - HB) * lax.axis_index("rep")
    before = (0, window[0])
    sent = []
    if window[0]:
        sent += begin(row_copies(disp, vel, disp_out, vel_out, sem, start, HB, HB, before))
    image = far_part(dense, halo, window)
    for i in range(HB):
        part = image[i * width : (i + 1) * width]
        finish_row(start + i, part, None, disp, vel, None, window)
        sent += begin(row_copies(disp, vel, disp_out, vel_out, sem, start + i, 1, i, window))
    end(sent)


def body(adj_disp, adj_vel, tangent_blocks, block_cols, inv_mass, joint_stiff, contact, states):
    rows, width, lanes = adj_disp.shape
    ring = lax.axis_size(RING)
    total = rows * ring
    inner, outer = ring_pairs(ring)
    pieces = lax.axis_size("ckpt")
    f32, bf16 = jnp.float32, jnp.bfloat16
    vm = pl.BlockSpec(memory_space=pltpu.VMEM)
    sm = pl.BlockSpec(memory_space=pltpu.SMEM)
    hbm = pl.BlockSpec(memory_space=pltpu.HBM)
    like = lambda a: pltpu.VMEM(a.shape, a.dtype)
    edge_t = pltpu.VMEM((HB, width, lanes), bf16)
    ext = pltpu.VMEM((rows + 2 * HB + 1, width, lanes), bf16)
    full = pltpu.VMEM((rows, width, lanes), f32)
    table = pltpu.VMEM((rows, width), f32)
    upright = pltpu.VMEM((WINDOW, width, rows), f32)
    dma = pltpu.SemaphoreType.DMA
    light = pl.CostEstimate(flops=1000, bytes_accessed=1000, transcendentals=0)
    heavy = pl.CostEstimate(flops=4_000_000_000, bytes_accessed=1000, transcendentals=0)
    adj_disp, adj_vel, tangent_blocks, cols, inv_mass, joint_stiff, contact, mine = (
        pltpu.with_memory_space_constraint(a, pltpu.HBM)
        for a in (
            adj_disp, adj_vel, tangent_blocks, block_cols.T, inv_mass, joint_stiff, contact, states
        )
    )

    def call(kernel, name, held, given, specs, made, made_specs, scratch=(), cost=light):
        return pl.pallas_call(
            kernel,
            name=name,
            out_shape=tuple(like(a) for a in held) + tuple(made),
            in_specs=[vm] * len(held) + list(specs),
            out_specs=(vm,) * len(held) + tuple(made_specs),
            input_output_aliases={i: i for i in range(len(held))},
            scratch_shapes=list(scratch),
            compiler_params=pltpu.CompilerParams(vmem_limit_bytes=VMEM_LIMIT),
            cost_estimate=cost,
        )(*held, *given)

    windows = windows_of(lanes)
    edges_t = [pltpu.VMEM((HB, width, size), bf16) for _, size in windows]

    out_b, *out_a = call(
        head, "head", [], [adj_vel, inv_mass], [hbm] * 2, [edge_t] + edges_t,
        [vm] * (len(windows) + 1), [edge_t, edge_t, table, dma((3,))],
    )
    states_late, out_a = lax.optimization_barrier((states, out_a))
    halo_a = [lax.ppermute(a, RING, inner) for a in out_a]
    whole_b = lax.ppermute(out_b, RING, outer)
    halo_b = [whole_b] * len(windows)
    others = [
        lax.ppermute(states_late, "ckpt", [((i + j) % pieces, i) for i in range(pieces)])
        for j in range(1, pieces)
    ]

    blocks, disp0, now, disp, vel, mass_b, bent, turned, place, dense = call(
        functools.partial(load_all, total), "load_all", [],
        [tangent_blocks, adj_vel, adj_disp, inv_mass, joint_stiff, contact, mine, cols], [hbm] * 8,
        [
            like(tangent_blocks), like(adj_disp), ext, full, full,
            pltpu.VMEM((rows, width, 128), f32), upright, upright, like(cols),
            pltpu.VMEM((HB * width, HB * width), bf16),
        ],
        [vm] * 10,
        [
            like(adj_vel), like(cols), pltpu.SMEM(cols.shape, jnp.int32), table, table,
            pltpu.VMEM(contact.shape, jnp.int32), pltpu.VMEM(states.shape, f32), dma((12,)),
        ],
    )
    blocks, disp0, now, disp, vel, mass_b, _, turned, *_, later, coeff, out_a = call(
        functools.partial(first_step, pieces), "first_step",
        [blocks, disp0, now, disp, vel, mass_b, bent, turned] + halo_a + others, [place], [sm],
        [ext, like(mass_b), edge_t], [vm] * 3,
    )
    halo_a = lax.ppermute(out_a, RING, inner)
    for step in range(WINDOW - 1, 0, -1):
        if step < WINDOW - 1:
            old = [disp0] if step == WINDOW - 2 else []
            blocks, later, disp, vel, mass_b, turned, coeff, _, now, *_, out_a = call(
                functools.partial(main_rows, step), "main_rows",
                [blocks, later, disp, vel, mass_b, turned, coeff, halo_a, now] + old,
                [place], [sm], [edge_t], [vm],
            )
            now, later = later, now
            halo_a = lax.ppermute(out_a, RING, inner)
        sent = []
        for n, window in enumerate(windows):
            dense, disp, vel, mass_b, halo, later, out = call(
                functools.partial(edge_rows, window), "edge_rows",
                [dense, disp, vel, mass_b, halo_b[n], later], [], [], [edges_t[n]], [vm],
                (), heavy if n else light,
            )
            sent.append(lax.ppermute(out, RING, outer))
            if step == WINDOW - 1:
                halo_b = [halo] * len(windows)
        halo_b = sent

    shape = jax.ShapeDtypeStruct((rows, width, lanes), f32)
    *_, disp, vel, _, _, _, disp_out, vel_out = call(
        main_last, "main_last", [blocks, later, disp, vel, turned, coeff, halo_a], [place], [sm],
        [shape] * 2, [hbm] * 2, [dma((2, rows // HB - 1))],
    )
    for window, halo in zip(windows[:-1], halo_b):
        dense, disp, vel, _ = call(
            functools.partial(edge_compute, window), "edge_compute",
            [dense, disp, vel, halo], [], [], [], [],
        )
    held = [dense, disp, vel, halo_b[-1]]
    return pl.pallas_call(
        functools.partial(edge_last, windows[-1]),
        name="edge_last",
        out_shape=tuple(like(a) for a in held) + (shape,) * 2,
        in_specs=[vm] * 4 + [hbm] * 2,
        out_specs=(vm,) * 4 + (hbm,) * 2,
        input_output_aliases={i: i for i in range(6)},
        scratch_shapes=[dma((2, HB + 1))],
        compiler_params=pltpu.CompilerParams(vmem_limit_bytes=VMEM_LIMIT),
        cost_estimate=light,
    )(*held, disp_out, vel_out)[-2:]


def solution(mesh):
    placed = (
        P(("groups", "space", "rep"), None, "ckpt"),
        P(("groups", "space", "rep"), None, "ckpt"),
        P(("groups", "space", "rep"), None, None),
        P(("groups", "space", "rep"), None),
        P(("groups", "space", "rep"), None),
        P(("groups", "space", "rep"), None),
        P(None, ("groups", "space", "rep")),
        P(None, ("groups", "space", "rep"), "ckpt"),
    )
    return jax.shard_map(
        body,
        mesh=mesh,
        in_specs=placed,
        out_specs=(
            P(("groups", "space", "rep"), None, "ckpt"),
            P(("groups", "space", "rep"), None, "ckpt"),
        ),
        check_vma=False,
    )
```

```python
import functools
import jax
import jax.numpy as jnp
from jax import lax
from jax.experimental import pallas as pl
from jax.experimental.pallas import tpu as pltpu
from jax.sharding import PartitionSpec as P

HB = 4
WINDOW = 3
RING = ("space", "rep")
VMEM_LIMIT = 24 * 1024 * 1024
LATE = 8


def ring_pairs(ring):
    inner = [(i, i ^ 1) for i in range(ring)]
    outer = [(i, (i + 1) % ring) for i in range(1, ring, 2)]
    outer = outer + [(b, a) for a, b in outer]
    return inner, outer


def windows_of(lanes):
    tiles = lanes // 128
    if tiles < 2:
        return [(0, lanes)]
    cut = 128 * ((tiles + 1) // 2)
    return [(0, cut), (cut, lanes - cut)]


def product(blocks, packed, place, r, window=None):
    slots = blocks.shape[2] // blocks.shape[1]
    at = slice(None) if window is None else pl.ds(*window)
    picked = jnp.concatenate([packed[place[k, r], :, at] for k in range(slots)], axis=0)
    return jnp.dot(blocks[r], picked, preferred_element_type=jnp.float32)


def tiled(column, lanes):
    return jnp.concatenate([column] * (lanes // 128), axis=1)


def spread(matrix, r, lanes):
    return jnp.broadcast_to(matrix[:, r : r + 1], (matrix.shape[0], lanes))


def each(count, one):
    def run(i, carry):
        one(i)
        return carry

    lax.fori_loop(0, count, run, 0, unroll=True)


def begin(copies):
    for c in copies:
        c.start()
    return copies


def end(copies):
    for c in copies:
        c.wait()


def head(vel0, inv_mass, *refs):
    out_b, *out_a, low, high, mass, sem = refs
    rows, _, lanes = vel0.shape
    rep = lax.axis_index("rep")
    loads = begin(
        [
            pltpu.make_async_copy(inv_mass, mass, sem.at[0]),
            pltpu.make_async_copy(vel0.at[pl.ds((rows - HB) * rep, HB)], low, sem.at[1]),
            pltpu.make_async_copy(vel0.at[pl.ds((rows - HB) * (1 - rep), HB)], high, sem.at[2]),
        ]
    )
    end(loads[:1])
    upright = 0.5 * mass[...].T
    first = [spread(upright, j, 128) for j in range(HB)]
    last = [spread(upright, rows - HB + j, 128) for j in range(HB)]
    mass_b = [jnp.where(rep == 0, p, q) for p, q in zip(first, last)]
    mass_a = [jnp.where(rep == 0, q, p) for p, q in zip(first, last)]
    end(loads[1:])
    for j in range(HB):
        out_b[j] = (tiled(mass_b[j], lanes) * low[j].astype(jnp.float32)).astype(jnp.bfloat16)
        a = (tiled(mass_a[j], lanes) * high[j].astype(jnp.float32)).astype(jnp.bfloat16)
        for ref, (at, size) in zip(out_a, windows_of(lanes)):
            ref[j] = a[:, at : at + size]


def load_all(total, blocks_in, vel0_in, disp0_in, inv_mass, stiff_in, contact_in, mine, cols_in, *refs):
    blocks, disp0, now, disp, vel, mass_b, bent, turned, place_out, dense = refs[:10]
    vel0, cols, place, mass, stiff, contact, shard, sem = refs[10:]
    rows, width, lanes = vel0.shape
    rep = lax.axis_index("rep")
    b_start = (rows - HB) * rep
    sides = (pl.ds(b_start, HB), pl.ds(HB, rows - 2 * HB), pl.ds((rows - HB) * (1 - rep), HB))
    get_cols = begin([pltpu.make_async_copy(cols_in, cols, sem.at[0])])
    small = begin(
        [
            pltpu.make_async_copy(inv_mass, mass, sem.at[1]),
            pltpu.make_async_copy(stiff_in, stiff, sem.at[2]),
            pltpu.make_async_copy(contact_in, contact, sem.at[3]),
            pltpu.make_async_copy(mine, shard, sem.at[4]),
        ]
    )
    get_vel = begin([pltpu.make_async_copy(vel0_in, vel0, sem.at[5])])
    get_rest = [
        begin(
            [
                pltpu.make_async_copy(blocks_in.at[at], blocks.at[at], sem.at[6 + 2 * n]),
                pltpu.make_async_copy(disp0_in.at[at], disp0.at[at], sem.at[7 + 2 * n]),
            ]
        )
        for n, at in enumerate(sides)
    ]
    now[rows + 2 * HB] = jnp.zeros(now.shape[1:], now.dtype)
    end(get_cols)
    first = (lax.axis_index("space") * 2 + rep) * rows
    row = lax.broadcasted_iota(jnp.int32, cols.shape, 1)
    off = cols[...] - (first + row)
    off = jnp.where(off > HB, off - total, off)
    off = jnp.where(off < -HB, off + total, off)
    place_out[...] = row + HB + off
    get_place = begin([pltpu.make_async_copy(place_out, place, sem.at[0])])
    end(small)
    upright = mass[...].T
    for r in range(rows):
        mass_b[r] = spread(upright, r, 128)
    part = shard.shape[2]
    home = pl.ds(pl.multiple_of(lax.axis_index("ckpt") * part, 8), part)
    stiff3 = 3.0 * stiff[...].T
    for s in range(WINDOW):
        bent[s] = stiff3 * contact[s : s + 1, :].astype(jnp.float32)
        turned[s, home, :] = shard[s].T
    end(get_vel)
    for r in range(rows):
        v = vel0[r].astype(jnp.float32)
        vel[r] = v
        now[r + HB] = (tiled(mass_b[r], lanes) * (0.5 * v)).astype(jnp.bfloat16)
    end(get_place)
    end(get_rest[0])
    slots = blocks.shape[2] // width
    shape = (width, HB * width)
    ahead = lax.broadcasted_iota(jnp.int32, shape, 1) - lax.broadcasted_iota(jnp.int32, shape, 0)
    for i in range(HB):
        r = b_start + i
        chosen = []
        for k in range(slots):
            j = place[k, r] - (rows + HB) * rep
            inside = jnp.logical_and(j >= 0, j < HB)
            at = jnp.where(inside, j * width, -width)
            chosen.append(jnp.where(ahead == at, 1.0, 0.0).astype(jnp.bfloat16))
        picked = jnp.dot(
            blocks[r], jnp.concatenate(chosen, axis=0), preferred_element_type=jnp.float32
        )
        dense[pl.ds(i * width, width), :] = picked.astype(jnp.bfloat16)
    for i in range(HB):
        r = b_start + i
        disp[r] = disp0[r].astype(jnp.float32) - near_product(i, blocks, now, place)
    end(get_rest[1])
    end(get_rest[2])


def finish_row(r, image, later, disp, vel, mass_b, window=None):
    at = slice(None) if window is None else pl.ds(*window)
    d = disp[r, :, at] - image
    v = vel[r, :, at] + d
    disp[r, :, at] = d
    vel[r, :, at] = v
    if later is not None:
        p = (tiled(mass_b[r], image.shape[1]) * v).astype(jnp.bfloat16)
        later[r + HB, :, at] = p
        return p


def joint(r, now, coeff):
    return tiled(coeff[r], now.shape[2]) * now[r + HB].astype(jnp.float32)


def spread_rows(matrix, out):
    for r in range(out.shape[0]):
        out[r] = spread(matrix, r, 128)


def near_product(i, blocks, now, place):
    rows = blocks.shape[0]
    rep = lax.axis_index("rep")
    r = (rows - HB) * rep + i
    low = (rows + HB) * rep
    slots = blocks.shape[2] // blocks.shape[1]
    picked = []
    for k in range(slots):
        p = place[k, r]
        inside = jnp.logical_and(p >= low, p < low + HB)
        picked.append(now[jnp.where(inside, rows + 2 * HB, p)])
    return jnp.dot(
        blocks[r], jnp.concatenate(picked, axis=0), preferred_element_type=jnp.float32
    )


def near_part(i, blocks, now, place, coeff, disp):
    rows = disp.shape[0]
    r = (rows - HB) * lax.axis_index("rep") + i
    disp[r] = disp[r] - (near_product(i, blocks, now, place) + joint(r, now, coeff))


def full_rows(start, count, blocks, now, later, disp_old, disp, vel, mass_b, coeff, place, out=None):
    def one(i):
        r = start + i
        if disp_old is not None:
            disp[r] = disp_old[r].astype(jnp.float32)
        image = product(blocks, now, place, r) + joint(r, now, coeff)
        p = finish_row(r, image, later, disp, vel, mass_b)
        if out is not None:
            out[i] = p

    each(count, one)


def first_step(pieces, *refs):
    held = (len(refs) - 4) // 2
    place = refs[held]
    blocks, disp0, now, disp, vel, mass_b, bent, turned, *halo = refs[held + 1 : -3 - (pieces - 1)]
    others = refs[-3 - (pieces - 1) : -3]
    later, coeff, out_a = refs[-3:]
    rows = disp.shape[0]
    part = turned.shape[1] // pieces
    me = lax.axis_index("ckpt")
    rep = lax.axis_index("rep")
    for s in range(WINDOW):
        for j, piece in enumerate(others):
            source = lax.rem(me + 1 + j, pieces)
            turned[s, pl.ds(pl.multiple_of(source * part, 8), part), :] = piece[s].T
        turned[s] = bent[s] * turned[s] * turned[s]
    spread_rows(turned[WINDOW - 1], coeff)
    later[rows + 2 * HB] = jnp.zeros(later.shape[1:], later.dtype)
    for j in range(HB):
        for ref, window in zip(halo, windows_of(now.shape[2])):
            now[(rows + HB) * (1 - rep) + j, :, pl.ds(*window)] = ref[j]
    state = (blocks, now, later, disp0, disp, vel, mass_b, coeff, place)
    full_rows((rows - HB) * (1 - rep), HB, *state, out_a)
    full_rows(HB, rows - 2 * HB - min(LATE, rows - 2 * HB), *state)
    for i in range(HB):
        r = (rows - HB) * rep + i
        disp[r] = disp[r] - joint(r, now, coeff)


def late_rows(*refs):
    place, blocks, disp0, now, later, disp, vel, mass_b, coeff = refs[-9:]
    rows = disp.shape[0]
    late = min(LATE, rows - 2 * HB)
    state = (blocks, now, later, disp0, disp, vel, mass_b, coeff, place)
    full_rows(rows - HB - late, late, *state)


def main_rows(step, *refs):
    place, blocks, now, disp, vel, mass_b, turned, coeff, halo, later, out = refs[-11:]
    rows = disp.shape[0]
    spread_rows(turned[step], coeff)
    side = 1 - lax.axis_index("rep")
    for j in range(HB):
        now[(rows + HB) * side + j] = halo[j]
    state = (blocks, now, later, None, disp, vel, mass_b, coeff, place)
    full_rows(HB * side, rows - HB, *state)
    for j in range(HB):
        out[j] = later[(rows - HB) * side + HB + j]
    each(HB, lambda i: near_part(i, blocks, now, place, coeff, disp))


def far_part(dense, halo, window):
    rows, width, lanes = halo.shape
    start, size = window
    start = start if lanes > size else 0
    seen = halo[:, :, start : start + size].reshape(rows * width, size)
    return jnp.dot(dense[...], seen, preferred_element_type=jnp.float32)


def edge_rows(window, *refs):
    dense, disp, vel, mass_b, halo, later, out = refs[-7:]
    rows, width, _ = disp.shape
    image = far_part(dense, halo, window)
    start = (rows - HB) * lax.axis_index("rep")
    for i in range(HB):
        part = image[i * width : (i + 1) * width]
        out[i] = finish_row(start + i, part, later, disp, vel, mass_b, window)


def row_copies(disp, vel, disp_out, vel_out, sem, start, count, g, window):
    at = (pl.ds(start, count), slice(None), pl.ds(*window))
    return [
        pltpu.make_async_copy(disp.at[at], disp_out.at[at], sem.at[0, g]),
        pltpu.make_async_copy(vel.at[at], vel_out.at[at], sem.at[1, g]),
    ]


def main_last(*refs):
    place, blocks, now, disp, vel, turned, coeff, halo, disp_out, vel_out, sem = refs[-11:]
    rows = disp.shape[0]
    spread_rows(turned[0], coeff)
    side = 1 - lax.axis_index("rep")
    for j in range(HB):
        now[(rows + HB) * side + j] = halo[j]
    sent = []
    for g in range(rows // HB - 1):
        start = HB * side + g * HB

        def one(i):
            r = start + i
            image = product(blocks, now, place, r) + joint(r, now, coeff)
            finish_row(r, image, None, disp, vel, None)

        each(HB, one)
        copies = row_copies(disp, vel, disp_out, vel_out, sem, start, HB, g, (0, disp.shape[2]))
        sent += begin(copies)
    each(HB, lambda i: near_part(i, blocks, now, place, coeff, disp))
    end(sent)


def edge_last(window, *refs):
    dense, disp, vel, halo, disp_out, vel_out, sem = refs[-7:]
    rows, width, _ = disp.shape
    start = (rows - HB) * lax.axis_index("rep")
    image = far_part(dense, halo, window)
    sent = []
    for i in range(HB):
        part = image[i * width : (i + 1) * width]
        finish_row(start + i, part, None, disp, vel, None, window)
        sent += begin(row_copies(disp, vel, disp_out, vel_out, sem, start + i, 1, i, window))
    end(sent)


def body(adj_disp, adj_vel, tangent_blocks, block_cols, inv_mass, joint_stiff, contact, states):
    rows, width, lanes = adj_disp.shape
    ring = lax.axis_size(RING)
    total = rows * ring
    inner, outer = ring_pairs(ring)
    pieces = lax.axis_size("ckpt")
    f32, bf16 = jnp.float32, jnp.bfloat16
    vm = pl.BlockSpec(memory_space=pltpu.VMEM)
    sm = pl.BlockSpec(memory_space=pltpu.SMEM)
    hbm = pl.BlockSpec(memory_space=pltpu.HBM)
    like = lambda a: pltpu.VMEM(a.shape, a.dtype)
    edge_t = pltpu.VMEM((HB, width, lanes), bf16)
    ext = pltpu.VMEM((rows + 2 * HB + 1, width, lanes), bf16)
    full = pltpu.VMEM((rows, width, lanes), f32)
    table = pltpu.VMEM((rows, width), f32)
    upright = pltpu.VMEM((WINDOW, width, rows), f32)
    dma = pltpu.SemaphoreType.DMA
    light = pl.CostEstimate(flops=1000, bytes_accessed=1000, transcendentals=0)
    heavy = pl.CostEstimate(flops=4_000_000_000, bytes_accessed=1000, transcendentals=0)
    adj_disp, adj_vel, tangent_blocks, cols, inv_mass, joint_stiff, contact, mine = (
        pltpu.with_memory_space_constraint(a, pltpu.HBM)
        for a in (
            adj_disp, adj_vel, tangent_blocks, block_cols.T, inv_mass, joint_stiff, contact, states
        )
    )

    def call(kernel, name, held, given, specs, made, made_specs, scratch=(), cost=light):
        return pl.pallas_call(
            kernel,
            name=name,
            out_shape=tuple(like(a) for a in held) + tuple(made),
            in_specs=[vm] * len(held) + list(specs),
            out_specs=(vm,) * len(held) + tuple(made_specs),
            input_output_aliases={i: i for i in range(len(held))},
            scratch_shapes=list(scratch),
            compiler_params=pltpu.CompilerParams(vmem_limit_bytes=VMEM_LIMIT),
            cost_estimate=cost,
        )(*held, *given)

    windows = windows_of(lanes)
    edges_t = [pltpu.VMEM((HB, width, size), bf16) for _, size in windows]

    out_b, *out_a = call(
        head, "head", [], [adj_vel, inv_mass], [hbm] * 2, [edge_t] + edges_t,
        [vm] * (len(windows) + 1), [edge_t, edge_t, table, dma((3,))],
    )
    states_late, out_a = lax.optimization_barrier((states, out_a))
    halo_a = [lax.ppermute(a, RING, inner) for a in out_a]
    whole_b = lax.ppermute(out_b, RING, outer)
    halo_b = [whole_b] * len(windows)
    others = [
        lax.ppermute(states_late, "ckpt", [((i + j) % pieces, i) for i in range(pieces)])
        for j in range(1, pieces)
    ]

    blocks, disp0, now, disp, vel, mass_b, bent, turned, place, dense = call(
        functools.partial(load_all, total), "load_all", [],
        [tangent_blocks, adj_vel, adj_disp, inv_mass, joint_stiff, contact, mine, cols], [hbm] * 8,
        [
            like(tangent_blocks), like(adj_disp), ext, full, full,
            pltpu.VMEM((rows, width, 128), f32), upright, upright, like(cols),
            pltpu.VMEM((HB * width, HB * width), bf16),
        ],
        [vm] * 10,
        [
            like(adj_vel), like(cols), pltpu.SMEM(cols.shape, jnp.int32), table, table,
            pltpu.VMEM(contact.shape, jnp.int32), pltpu.VMEM(states.shape, f32), dma((12,)),
        ],
    )
    blocks, disp0, now, disp, vel, mass_b, _, turned, *_, later, coeff, out_a = call(
        functools.partial(first_step, pieces), "first_step",
        [blocks, disp0, now, disp, vel, mass_b, bent, turned] + halo_a + others, [place], [sm],
        [ext, like(mass_b), edge_t], [vm] * 3,
    )
    halo_a = lax.ppermute(out_a, RING, inner)
    for step in range(WINDOW - 1, 0, -1):
        if step < WINDOW - 1:
            blocks, later, disp, vel, mass_b, turned, coeff, _, now, out_a = call(
                functools.partial(main_rows, step), "main_rows",
                [blocks, later, disp, vel, mass_b, turned, coeff, halo_a, now],
                [place], [sm], [edge_t], [vm],
            )
            now, later = later, now
            halo_a = lax.ppermute(out_a, RING, inner)
        sent = []
        for n, window in enumerate(windows):
            dense, disp, vel, mass_b, halo, later, out = call(
                functools.partial(edge_rows, window), "edge_rows",
                [dense, disp, vel, mass_b, halo_b[n], later], [], [], [edges_t[n]], [vm],
                (), heavy if n else light,
            )
            sent.append(lax.ppermute(out, RING, outer))
            if step == WINDOW - 1:
                halo_b = [halo] * len(windows)
                if n == 0:
                    blocks, _, now, later, disp, vel, mass_b, coeff = call(
                        late_rows, "late_rows",
                        [blocks, disp0, now, later, disp, vel, mass_b, coeff], [place], [sm],
                        [], [],
                    )
        halo_b = sent

    shape = jax.ShapeDtypeStruct((rows, width, lanes), f32)
    *_, disp, vel, _, _, _, disp_out, vel_out = call(
        main_last, "main_last", [blocks, later, disp, vel, turned, coeff, halo_a], [place], [sm],
        [shape] * 2, [hbm] * 2, [dma((2, rows // HB - 1))],
    )
    for window, halo in zip(windows, halo_b):
        held = [dense, disp, vel, halo]
        dense, disp, vel, _, disp_out, vel_out = pl.pallas_call(
            functools.partial(edge_last, window),
            name="edge_last",
            out_shape=tuple(like(a) for a in held) + (shape,) * 2,
            in_specs=[vm] * 4 + [hbm] * 2,
            out_specs=(vm,) * 4 + (hbm,) * 2,
            input_output_aliases={i: i for i in range(6)},
            scratch_shapes=[dma((2, HB))],
            compiler_params=pltpu.CompilerParams(vmem_limit_bytes=VMEM_LIMIT),
            cost_estimate=light,
        )(*held, disp_out, vel_out)
    return disp_out, vel_out


def solution(mesh):
    placed = (
        P(("groups", "space", "rep"), None, "ckpt"),
        P(("groups", "space", "rep"), None, "ckpt"),
        P(("groups", "space", "rep"), None, None),
        P(("groups", "space", "rep"), None),
        P(("groups", "space", "rep"), None),
        P(("groups", "space", "rep"), None),
        P(None, ("groups", "space", "rep")),
        P(None, ("groups", "space", "rep"), "ckpt"),
    )
    return jax.shard_map(
        body,
        mesh=mesh,
        in_specs=placed,
        out_specs=(
            P(("groups", "space", "rep"), None, "ckpt"),
            P(("groups", "space", "rep"), None, "ckpt"),
        ),
        check_vma=False,
    )
```

```python
import functools
import jax
import jax.numpy as jnp
from jax import lax
from jax.experimental import pallas as pl
from jax.experimental.pallas import tpu as pltpu
from jax.sharding import PartitionSpec as P

HB = 4
WINDOW = 3
RING = ("space", "rep")
VMEM_LIMIT = 24 * 1024 * 1024
LATE = 10


def ring_pairs(ring):
    inner = [(i, i ^ 1) for i in range(ring)]
    outer = [(i, (i + 1) % ring) for i in range(1, ring, 2)]
    outer = outer + [(b, a) for a, b in outer]
    return inner, outer


def windows_of(lanes):
    tiles = lanes // 128
    if tiles < 2:
        return [(0, lanes)]
    cut = 128 * ((tiles + 1) // 2)
    return [(0, cut), (cut, lanes - cut)]


def product(blocks, packed, place, r, window=None):
    slots = blocks.shape[2] // blocks.shape[1]
    at = slice(None) if window is None else pl.ds(*window)
    picked = jnp.concatenate([packed[place[k, r], :, at] for k in range(slots)], axis=0)
    return jnp.dot(blocks[r], picked, preferred_element_type=jnp.float32)


def tiled(column, lanes):
    return jnp.concatenate([column] * (lanes // 128), axis=1)


def spread(matrix, r, lanes):
    return jnp.broadcast_to(matrix[:, r : r + 1], (matrix.shape[0], lanes))


def each(count, one):
    def run(i, carry):
        one(i)
        return carry

    lax.fori_loop(0, count, run, 0, unroll=True)


def begin(copies):
    for c in copies:
        c.start()
    return copies


def end(copies):
    for c in copies:
        c.wait()


def head(vel0, inv_mass, *refs):
    out_b, *out_a, low, high, mass, sem = refs
    rows, _, lanes = vel0.shape
    rep = lax.axis_index("rep")
    loads = begin(
        [
            pltpu.make_async_copy(inv_mass, mass, sem.at[0]),
            pltpu.make_async_copy(vel0.at[pl.ds((rows - HB) * rep, HB)], low, sem.at[1]),
            pltpu.make_async_copy(vel0.at[pl.ds((rows - HB) * (1 - rep), HB)], high, sem.at[2]),
        ]
    )
    end(loads[:1])
    upright = 0.5 * mass[...].T
    first = [spread(upright, j, 128) for j in range(HB)]
    last = [spread(upright, rows - HB + j, 128) for j in range(HB)]
    mass_b = [jnp.where(rep == 0, p, q) for p, q in zip(first, last)]
    mass_a = [jnp.where(rep == 0, q, p) for p, q in zip(first, last)]
    end(loads[1:])
    for j in range(HB):
        out_b[j] = (tiled(mass_b[j], lanes) * low[j].astype(jnp.float32)).astype(jnp.bfloat16)
        a = (tiled(mass_a[j], lanes) * high[j].astype(jnp.float32)).astype(jnp.bfloat16)
        for ref, (at, size) in zip(out_a, windows_of(lanes)):
            ref[j] = a[:, at : at + size]


def load_all(total, blocks_in, vel0_in, disp0_in, inv_mass, stiff_in, contact_in, mine, cols_in, *refs):
    blocks, disp0, now, disp, vel, mass_b, bent, turned, place_out, dense = refs[:10]
    vel0, cols, place, mass, stiff, contact, shard, sem = refs[10:]
    rows, width, lanes = vel0.shape
    rep = lax.axis_index("rep")
    b_start = (rows - HB) * rep
    sides = (pl.ds(b_start, HB), pl.ds(HB, rows - 2 * HB), pl.ds((rows - HB) * (1 - rep), HB))
    get_cols = begin([pltpu.make_async_copy(cols_in, cols, sem.at[0])])
    small = begin(
        [
            pltpu.make_async_copy(inv_mass, mass, sem.at[1]),
            pltpu.make_async_copy(stiff_in, stiff, sem.at[2]),
            pltpu.make_async_copy(contact_in, contact, sem.at[3]),
            pltpu.make_async_copy(mine, shard, sem.at[4]),
        ]
    )
    get_vel = begin([pltpu.make_async_copy(vel0_in, vel0, sem.at[5])])
    get_rest = [
        begin(
            [
                pltpu.make_async_copy(blocks_in.at[at], blocks.at[at], sem.at[6 + 2 * n]),
                pltpu.make_async_copy(disp0_in.at[at], disp0.at[at], sem.at[7 + 2 * n]),
            ]
        )
        for n, at in enumerate(sides)
    ]
    now[rows + 2 * HB] = jnp.zeros(now.shape[1:], now.dtype)
    end(get_cols)
    first = (lax.axis_index("space") * 2 + rep) * rows
    row = lax.broadcasted_iota(jnp.int32, cols.shape, 1)
    off = cols[...] - (first + row)
    off = jnp.where(off > HB, off - total, off)
    off = jnp.where(off < -HB, off + total, off)
    place_out[...] = row + HB + off
    get_place = begin([pltpu.make_async_copy(place_out, place, sem.at[0])])
    end(small)
    upright = mass[...].T
    for r in range(rows):
        mass_b[r] = spread(upright, r, 128)
    part = shard.shape[2]
    home = pl.ds(pl.multiple_of(lax.axis_index("ckpt") * part, 8), part)
    stiff3 = 3.0 * stiff[...].T
    for s in range(WINDOW):
        bent[s] = stiff3 * contact[s : s + 1, :].astype(jnp.float32)
        turned[s, home, :] = shard[s].T
    end(get_vel)
    for r in range(rows):
        v = vel0[r].astype(jnp.float32)
        vel[r] = v
        now[r + HB] = (tiled(mass_b[r], lanes) * (0.5 * v)).astype(jnp.bfloat16)
    end(get_place)
    end(get_rest[0])
    slots = blocks.shape[2] // width
    shape = (width, HB * width)
    ahead = lax.broadcasted_iota(jnp.int32, shape, 1) - lax.broadcasted_iota(jnp.int32, shape, 0)
    for i in range(HB):
        r = b_start + i
        chosen = []
        for k in range(slots):
            j = place[k, r] - (rows + HB) * rep
            inside = jnp.logical_and(j >= 0, j < HB)
            at = jnp.where(inside, j * width, -width)
            chosen.append(jnp.where(ahead == at, 1.0, 0.0).astype(jnp.bfloat16))
        picked = jnp.dot(
            blocks[r], jnp.concatenate(chosen, axis=0), preferred_element_type=jnp.float32
        )
        dense[pl.ds(i * width, width), :] = picked.astype(jnp.bfloat16)
    for i in range(HB):
        r = b_start + i
        disp[r] = disp0[r].astype(jnp.float32) - near_product(i, blocks, now, place)
    end(get_rest[1])
    end(get_rest[2])


def finish_row(r, image, later, disp, vel, mass_b, window=None):
    at = slice(None) if window is None else pl.ds(*window)
    d = disp[r, :, at] - image
    v = vel[r, :, at] + d
    disp[r, :, at] = d
    vel[r, :, at] = v
    if later is not None:
        p = (tiled(mass_b[r], image.shape[1]) * v).astype(jnp.bfloat16)
        later[r + HB, :, at] = p
        return p


def joint(r, now, coeff):
    return tiled(coeff[r], now.shape[2]) * now[r + HB].astype(jnp.float32)


def spread_rows(matrix, out):
    for r in range(out.shape[0]):
        out[r] = spread(matrix, r, 128)


def near_product(i, blocks, now, place):
    rows = blocks.shape[0]
    rep = lax.axis_index("rep")
    r = (rows - HB) * rep + i
    low = (rows + HB) * rep
    slots = blocks.shape[2] // blocks.shape[1]
    picked = []
    for k in range(slots):
        p = place[k, r]
        inside = jnp.logical_and(p >= low, p < low + HB)
        picked.append(now[jnp.where(inside, rows + 2 * HB, p)])
    return jnp.dot(
        blocks[r], jnp.concatenate(picked, axis=0), preferred_element_type=jnp.float32
    )


def near_part(i, blocks, now, place, coeff, disp):
    rows = disp.shape[0]
    r = (rows - HB) * lax.axis_index("rep") + i
    disp[r] = disp[r] - (near_product(i, blocks, now, place) + joint(r, now, coeff))


def full_rows(start, count, blocks, now, later, disp_old, disp, vel, mass_b, coeff, place, out=None):
    def one(i):
        r = start + i
        if disp_old is not None:
            disp[r] = disp_old[r].astype(jnp.float32)
        image = product(blocks, now, place, r) + joint(r, now, coeff)
        p = finish_row(r, image, later, disp, vel, mass_b)
        if out is not None:
            out[i] = p

    each(count, one)


def first_step(pieces, *refs):
    held = (len(refs) - 4) // 2
    place = refs[held]
    blocks, disp0, now, disp, vel, mass_b, bent, turned, *halo = refs[held + 1 : -3 - (pieces - 1)]
    others = refs[-3 - (pieces - 1) : -3]
    later, coeff, out_a = refs[-3:]
    rows = disp.shape[0]
    part = turned.shape[1] // pieces
    me = lax.axis_index("ckpt")
    rep = lax.axis_index("rep")
    for s in range(WINDOW):
        for j, piece in enumerate(others):
            source = lax.rem(me + 1 + j, pieces)
            turned[s, pl.ds(pl.multiple_of(source * part, 8), part), :] = piece[s].T
        turned[s] = bent[s] * turned[s] * turned[s]
    for s in range(WINDOW):
        spread_rows(turned[s], coeff.at[s])
    coeff = coeff.at[WINDOW - 1]
    later[rows + 2 * HB] = jnp.zeros(later.shape[1:], later.dtype)
    for j in range(HB):
        for ref, window in zip(halo, windows_of(now.shape[2])):
            now[(rows + HB) * (1 - rep) + j, :, pl.ds(*window)] = ref[j]
    state = (blocks, now, later, disp0, disp, vel, mass_b, coeff, place)
    full_rows((rows - HB) * (1 - rep), HB, *state, out_a)
    full_rows(HB, rows - 2 * HB - min(LATE, rows - 2 * HB), *state)
    for i in range(HB):
        r = (rows - HB) * rep + i
        disp[r] = disp[r] - joint(r, now, coeff)


def late_rows(*refs):
    place, blocks, disp0, now, later, disp, vel, mass_b, coeff = refs[-9:]
    rows = disp.shape[0]
    late = min(LATE, rows - 2 * HB)
    state = (blocks, now, later, disp0, disp, vel, mass_b, coeff.at[WINDOW - 1], place)
    full_rows(rows - HB - late, late, *state)


def main_rows(step, *refs):
    place, blocks, now, disp, vel, mass_b, turned, coeff, halo, later, out = refs[-11:]
    rows = disp.shape[0]
    coeff = coeff.at[step]
    side = 1 - lax.axis_index("rep")
    for j in range(HB):
        now[(rows + HB) * side + j] = halo[j]
    state = (blocks, now, later, None, disp, vel, mass_b, coeff, place)
    full_rows(HB * side, rows - HB, *state)
    for j in range(HB):
        out[j] = later[(rows - HB) * side + HB + j]
    each(HB, lambda i: near_part(i, blocks, now, place, coeff, disp))


def far_part(dense, halo, window):
    rows, width, lanes = halo.shape
    start, size = window
    start = start if lanes > size else 0
    seen = halo[:, :, start : start + size].reshape(rows * width, size)
    return jnp.dot(dense[...], seen, preferred_element_type=jnp.float32)


def edge_rows(window, *refs):
    dense, disp, vel, mass_b, halo, later, out = refs[-7:]
    rows, width, _ = disp.shape
    image = far_part(dense, halo, window)
    start = (rows - HB) * lax.axis_index("rep")
    for i in range(HB):
        part = image[i * width : (i + 1) * width]
        out[i] = finish_row(start + i, part, later, disp, vel, mass_b, window)


def row_copies(disp, vel, disp_out, vel_out, sem, start, count, g, window):
    at = (pl.ds(start, count), slice(None), pl.ds(*window))
    return [
        pltpu.make_async_copy(disp.at[at], disp_out.at[at], sem.at[0, g]),
        pltpu.make_async_copy(vel.at[at], vel_out.at[at], sem.at[1, g]),
    ]


def main_last(*refs):
    place, blocks, now, disp, vel, turned, coeff, halo, disp_out, vel_out, sem = refs[-11:]
    rows = disp.shape[0]
    coeff = coeff.at[0]
    side = 1 - lax.axis_index("rep")
    for j in range(HB):
        now[(rows + HB) * side + j] = halo[j]
    sent = []
    for g in range(rows // HB - 1):
        start = HB * side + g * HB

        def one(i):
            r = start + i
            image = product(blocks, now, place, r) + joint(r, now, coeff)
            finish_row(r, image, None, disp, vel, None)

        each(HB, one)
        copies = row_copies(disp, vel, disp_out, vel_out, sem, start, HB, g, (0, disp.shape[2]))
        sent += begin(copies)
    each(HB, lambda i: near_part(i, blocks, now, place, coeff, disp))
    end(sent)


def edge_last(window, *refs):
    dense, disp, vel, halo, disp_out, vel_out, sem = refs[-7:]
    rows, width, _ = disp.shape
    start = (rows - HB) * lax.axis_index("rep")
    image = far_part(dense, halo, window)
    sent = []
    for i in range(HB):
        part = image[i * width : (i + 1) * width]
        finish_row(start + i, part, None, disp, vel, None, window)
        sent += begin(row_copies(disp, vel, disp_out, vel_out, sem, start + i, 1, i, window))
    end(sent)


def body(adj_disp, adj_vel, tangent_blocks, block_cols, inv_mass, joint_stiff, contact, states):
    rows, width, lanes = adj_disp.shape
    ring = lax.axis_size(RING)
    total = rows * ring
    inner, outer = ring_pairs(ring)
    pieces = lax.axis_size("ckpt")
    f32, bf16 = jnp.float32, jnp.bfloat16
    vm = pl.BlockSpec(memory_space=pltpu.VMEM)
    sm = pl.BlockSpec(memory_space=pltpu.SMEM)
    hbm = pl.BlockSpec(memory_space=pltpu.HBM)
    like = lambda a: pltpu.VMEM(a.shape, a.dtype)
    edge_t = pltpu.VMEM((HB, width, lanes), bf16)
    ext = pltpu.VMEM((rows + 2 * HB + 1, width, lanes), bf16)
    full = pltpu.VMEM((rows, width, lanes), f32)
    table = pltpu.VMEM((rows, width), f32)
    upright = pltpu.VMEM((WINDOW, width, rows), f32)
    dma = pltpu.SemaphoreType.DMA
    light = pl.CostEstimate(flops=1000, bytes_accessed=1000, transcendentals=0)
    heavy = pl.CostEstimate(flops=4_000_000_000, bytes_accessed=1000, transcendentals=0)
    adj_disp, adj_vel, tangent_blocks, cols, inv_mass, joint_stiff, contact, mine = (
        pltpu.with_memory_space_constraint(a, pltpu.HBM)
        for a in (
            adj_disp, adj_vel, tangent_blocks, block_cols.T, inv_mass, joint_stiff, contact, states
        )
    )

    def call(kernel, name, held, given, specs, made, made_specs, scratch=(), cost=light):
        return pl.pallas_call(
            kernel,
            name=name,
            out_shape=tuple(like(a) for a in held) + tuple(made),
            in_specs=[vm] * len(held) + list(specs),
            out_specs=(vm,) * len(held) + tuple(made_specs),
            input_output_aliases={i: i for i in range(len(held))},
            scratch_shapes=list(scratch),
            compiler_params=pltpu.CompilerParams(vmem_limit_bytes=VMEM_LIMIT),
            cost_estimate=cost,
        )(*held, *given)

    windows = windows_of(lanes)
    edges_t = [pltpu.VMEM((HB, width, size), bf16) for _, size in windows]

    out_b, *out_a = call(
        head, "head", [], [adj_vel, inv_mass], [hbm] * 2, [edge_t] + edges_t,
        [vm] * (len(windows) + 1), [edge_t, edge_t, table, dma((3,))],
    )
    states_late, out_a = lax.optimization_barrier((states, out_a))
    halo_a = [lax.ppermute(a, RING, inner) for a in out_a]
    whole_b = lax.ppermute(out_b, RING, outer)
    halo_b = [whole_b] * len(windows)
    others = [
        lax.ppermute(states_late, "ckpt", [((i + j) % pieces, i) for i in range(pieces)])
        for j in range(1, pieces)
    ]

    blocks, disp0, now, disp, vel, mass_b, bent, turned, place, dense = call(
        functools.partial(load_all, total), "load_all", [],
        [tangent_blocks, adj_vel, adj_disp, inv_mass, joint_stiff, contact, mine, cols], [hbm] * 8,
        [
            like(tangent_blocks), like(adj_disp), ext, full, full,
            pltpu.VMEM((rows, width, 128), f32), upright, upright, like(cols),
            pltpu.VMEM((HB * width, HB * width), bf16),
        ],
        [vm] * 10,
        [
            like(adj_vel), like(cols), pltpu.SMEM(cols.shape, jnp.int32), table, table,
            pltpu.VMEM(contact.shape, jnp.int32), pltpu.VMEM(states.shape, f32), dma((12,)),
        ],
    )
    blocks, disp0, now, disp, vel, mass_b, _, turned, *_, later, coeff, out_a = call(
        functools.partial(first_step, pieces), "first_step",
        [blocks, disp0, now, disp, vel, mass_b, bent, turned] + halo_a + others, [place], [sm],
        [ext, pltpu.VMEM((WINDOW, rows, width, 128), f32), edge_t], [vm] * 3,
    )
    halo_a = lax.ppermute(out_a, RING, inner)
    for step in range(WINDOW - 1, 0, -1):
        if step < WINDOW - 1:
            blocks, later, disp, vel, mass_b, turned, coeff, _, now, out_a = call(
                functools.partial(main_rows, step), "main_rows",
                [blocks, later, disp, vel, mass_b, turned, coeff, halo_a, now],
                [place], [sm], [edge_t], [vm],
            )
            now, later = later, now
            halo_a = lax.ppermute(out_a, RING, inner)
        sent = []
        for n, window in enumerate(windows):
            dense, disp, vel, mass_b, halo, later, out = call(
                functools.partial(edge_rows, window), "edge_rows",
                [dense, disp, vel, mass_b, halo_b[n], later], [], [], [edges_t[n]], [vm],
                (), heavy if n else light,
            )
            sent.append(lax.ppermute(out, RING, outer))
            if step == WINDOW - 1:
                halo_b = [halo] * len(windows)
                if n == 0:
                    blocks, _, now, later, disp, vel, mass_b, coeff = call(
                        late_rows, "late_rows",
                        [blocks, disp0, now, later, disp, vel, mass_b, coeff], [place], [sm],
                        [], [],
                    )
        halo_b = sent

    shape = jax.ShapeDtypeStruct((rows, width, lanes), f32)
    *_, disp, vel, _, _, _, disp_out, vel_out = call(
        main_last, "main_last", [blocks, later, disp, vel, turned, coeff, halo_a], [place], [sm],
        [shape] * 2, [hbm] * 2, [dma((2, rows // HB - 1))],
    )
    for window, halo in zip(windows, halo_b):
        held = [dense, disp, vel, halo]
        dense, disp, vel, _, disp_out, vel_out = pl.pallas_call(
            functools.partial(edge_last, window),
            name="edge_last",
            out_shape=tuple(like(a) for a in held) + (shape,) * 2,
            in_specs=[vm] * 4 + [hbm] * 2,
            out_specs=(vm,) * 4 + (hbm,) * 2,
            input_output_aliases={i: i for i in range(6)},
            scratch_shapes=[dma((2, HB))],
            compiler_params=pltpu.CompilerParams(vmem_limit_bytes=VMEM_LIMIT),
            cost_estimate=light,
        )(*held, disp_out, vel_out)
    return disp_out, vel_out


def solution(mesh):
    placed = (
        P(("groups", "space", "rep"), None, "ckpt"),
        P(("groups", "space", "rep"), None, "ckpt"),
        P(("groups", "space", "rep"), None, None),
        P(("groups", "space", "rep"), None),
        P(("groups", "space", "rep"), None),
        P(("groups", "space", "rep"), None),
        P(None, ("groups", "space", "rep")),
        P(None, ("groups", "space", "rep"), "ckpt"),
    )
    return jax.shard_map(
        body,
        mesh=mesh,
        in_specs=placed,
        out_specs=(
            P(("groups", "space", "rep"), None, "ckpt"),
            P(("groups", "space", "rep"), None, "ckpt"),
        ),
        check_vma=False,
    )
```

```python
import functools
import jax
import jax.numpy as jnp
from jax import lax
from jax.experimental import pallas as pl
from jax.experimental.pallas import tpu as pltpu
from jax.sharding import PartitionSpec as P

HB = 4
WINDOW = 3
RING = ("space", "rep")
VMEM_LIMIT = 24 * 1024 * 1024
LATE = 10


def ring_pairs(ring):
    inner = [(i, i ^ 1) for i in range(ring)]
    outer = [(i, (i + 1) % ring) for i in range(1, ring, 2)]
    outer = outer + [(b, a) for a, b in outer]
    return inner, outer


def windows_of(lanes):
    tiles = lanes // 128
    if tiles < 2:
        return [(0, lanes)]
    cut = 128 * ((tiles + 1) // 2)
    return [(0, cut), (cut, lanes - cut)]


def product(blocks, packed, place, r, window=None):
    slots = blocks.shape[2] // blocks.shape[1]
    at = slice(None) if window is None else pl.ds(*window)
    picked = jnp.concatenate([packed[place[k, r], :, at] for k in range(slots)], axis=0)
    return jnp.dot(blocks[r], picked, preferred_element_type=jnp.float32)


def tiled(column, lanes):
    return jnp.concatenate([column] * (lanes // 128), axis=1)


def spread(matrix, r, lanes):
    return jnp.broadcast_to(matrix[:, r : r + 1], (matrix.shape[0], lanes))


def each(count, one):
    def run(i, carry):
        one(i)
        return carry

    lax.fori_loop(0, count, run, 0, unroll=True)


def begin(copies):
    for c in copies:
        c.start()
    return copies


def end(copies):
    for c in copies:
        c.wait()


def head(vel0, inv_mass, *refs):
    out_b, *out_a, low, high, mass, sem = refs
    rows, _, lanes = vel0.shape
    rep = lax.axis_index("rep")
    loads = begin(
        [
            pltpu.make_async_copy(inv_mass, mass, sem.at[0]),
            pltpu.make_async_copy(vel0.at[pl.ds((rows - HB) * rep, HB)], low, sem.at[1]),
            pltpu.make_async_copy(vel0.at[pl.ds((rows - HB) * (1 - rep), HB)], high, sem.at[2]),
        ]
    )
    end(loads[:1])
    upright = 0.5 * mass[...].T
    first = [spread(upright, j, 128) for j in range(HB)]
    last = [spread(upright, rows - HB + j, 128) for j in range(HB)]
    mass_b = [jnp.where(rep == 0, p, q) for p, q in zip(first, last)]
    mass_a = [jnp.where(rep == 0, q, p) for p, q in zip(first, last)]
    end(loads[1:])
    for j in range(HB):
        out_b[j] = (tiled(mass_b[j], lanes) * low[j].astype(jnp.float32)).astype(jnp.bfloat16)
        a = (tiled(mass_a[j], lanes) * high[j].astype(jnp.float32)).astype(jnp.bfloat16)
        for ref, (at, size) in zip(out_a, windows_of(lanes)):
            ref[j] = a[:, at : at + size]


def load_all(total, blocks_in, vel0_in, disp0_in, inv_mass, stiff_in, contact_in, mine, cols_in, *refs):
    blocks, disp0, now, disp, vel, mass_b, bent, turned, place_out, dense = refs[:10]
    vel0, cols, place, mass, stiff, contact, shard, sem = refs[10:]
    rows, width, lanes = vel0.shape
    rep = lax.axis_index("rep")
    b_start = (rows - HB) * rep
    sides = (pl.ds(b_start, HB), pl.ds(HB, rows - 2 * HB), pl.ds((rows - HB) * (1 - rep), HB))
    get_cols = begin([pltpu.make_async_copy(cols_in, cols, sem.at[0])])
    small = begin(
        [
            pltpu.make_async_copy(inv_mass, mass, sem.at[1]),
            pltpu.make_async_copy(stiff_in, stiff, sem.at[2]),
            pltpu.make_async_copy(contact_in, contact, sem.at[3]),
            pltpu.make_async_copy(mine, shard, sem.at[4]),
        ]
    )
    get_vel = begin([pltpu.make_async_copy(vel0_in, vel0, sem.at[5])])
    get_rest = [
        begin(
            [
                pltpu.make_async_copy(blocks_in.at[at], blocks.at[at], sem.at[6 + 2 * n]),
                pltpu.make_async_copy(disp0_in.at[at], disp0.at[at], sem.at[7 + 2 * n]),
            ]
        )
        for n, at in enumerate(sides)
    ]
    now[rows + 2 * HB] = jnp.zeros(now.shape[1:], now.dtype)
    end(get_cols)
    first = (lax.axis_index("space") * 2 + rep) * rows
    row = lax.broadcasted_iota(jnp.int32, cols.shape, 1)
    off = cols[...] - (first + row)
    off = jnp.where(off > HB, off - total, off)
    off = jnp.where(off < -HB, off + total, off)
    place_out[...] = row + HB + off
    get_place = begin([pltpu.make_async_copy(place_out, place, sem.at[0])])
    end(small)
    upright = mass[...].T
    for r in range(rows):
        mass_b[r] = spread(upright, r, 128)
    part = shard.shape[2]
    home = pl.ds(pl.multiple_of(lax.axis_index("ckpt") * part, 8), part)
    stiff3 = 3.0 * stiff[...].T
    for s in range(WINDOW):
        bent[s] = stiff3 * contact[s : s + 1, :].astype(jnp.float32)
        turned[s, home, :] = shard[s].T
    end(get_vel)
    for r in range(rows):
        v = vel0[r].astype(jnp.float32)
        vel[r] = v
        now[r + HB] = (tiled(mass_b[r], lanes) * (0.5 * v)).astype(jnp.bfloat16)
    end(get_place)
    end(get_rest[0])
    slots = blocks.shape[2] // width
    shape = (width, HB * width)
    ahead = lax.broadcasted_iota(jnp.int32, shape, 1) - lax.broadcasted_iota(jnp.int32, shape, 0)
    for i in range(HB):
        r = b_start + i
        chosen = []
        for k in range(slots):
            j = place[k, r] - (rows + HB) * rep
            inside = jnp.logical_and(j >= 0, j < HB)
            at = jnp.where(inside, j * width, -width)
            chosen.append(jnp.where(ahead == at, 1.0, 0.0).astype(jnp.bfloat16))
        picked = jnp.dot(
            blocks[r], jnp.concatenate(chosen, axis=0), preferred_element_type=jnp.float32
        )
        dense[pl.ds(i * width, width), :] = picked.astype(jnp.bfloat16)
    for i in range(HB):
        r = b_start + i
        disp[r] = disp0[r].astype(jnp.float32) - near_product(i, blocks, now, place)
    end(get_rest[1])
    end(get_rest[2])


def finish_row(r, image, later, disp, vel, mass_b, window=None):
    at = slice(None) if window is None else pl.ds(*window)
    d = disp[r, :, at] - image
    v = vel[r, :, at] + d
    disp[r, :, at] = d
    vel[r, :, at] = v
    if later is not None:
        p = (tiled(mass_b[r], image.shape[1]) * v).astype(jnp.bfloat16)
        later[r + HB, :, at] = p
        return p


def joint(r, now, coeff):
    return tiled(coeff[r], now.shape[2]) * now[r + HB].astype(jnp.float32)


def spread_rows(matrix, out):
    for r in range(out.shape[0]):
        out[r] = spread(matrix, r, 128)


def near_product(i, blocks, now, place):
    rows = blocks.shape[0]
    rep = lax.axis_index("rep")
    r = (rows - HB) * rep + i
    low = (rows + HB) * rep
    slots = blocks.shape[2] // blocks.shape[1]
    picked = []
    for k in range(slots):
        p = place[k, r]
        inside = jnp.logical_and(p >= low, p < low + HB)
        picked.append(now[jnp.where(inside, rows + 2 * HB, p)])
    return jnp.dot(
        blocks[r], jnp.concatenate(picked, axis=0), preferred_element_type=jnp.float32
    )


def near_part(i, blocks, now, place, coeff, disp):
    rows = disp.shape[0]
    r = (rows - HB) * lax.axis_index("rep") + i
    disp[r] = disp[r] - (near_product(i, blocks, now, place) + joint(r, now, coeff))


def full_rows(start, count, blocks, now, later, disp_old, disp, vel, mass_b, coeff, place, out=None):
    def one(i):
        r = start + i
        if disp_old is not None:
            disp[r] = disp_old[r].astype(jnp.float32)
        image = product(blocks, now, place, r) + joint(r, now, coeff)
        p = finish_row(r, image, later, disp, vel, mass_b)
        if out is not None:
            out[i] = p

    each(count, one)


def first_step(pieces, *refs):
    held = (len(refs) - 4) // 2
    place = refs[held]
    blocks, disp0, now, disp, vel, mass_b, bent, turned, *halo = refs[held + 1 : -3 - (pieces - 1)]
    others = refs[-3 - (pieces - 1) : -3]
    later, coeff, out_a = refs[-3:]
    rows = disp.shape[0]
    part = turned.shape[1] // pieces
    me = lax.axis_index("ckpt")
    rep = lax.axis_index("rep")
    for s in range(WINDOW):
        for j, piece in enumerate(others):
            source = lax.rem(me + 1 + j, pieces)
            turned[s, pl.ds(pl.multiple_of(source * part, 8), part), :] = piece[s].T
        turned[s] = bent[s] * turned[s] * turned[s]
    for s in range(WINDOW):
        spread_rows(turned[s], coeff.at[s])
    coeff = coeff.at[WINDOW - 1]
    later[rows + 2 * HB] = jnp.zeros(later.shape[1:], later.dtype)
    for j in range(HB):
        for ref, window in zip(halo, windows_of(now.shape[2])):
            now[(rows + HB) * (1 - rep) + j, :, pl.ds(*window)] = ref[j]
    state = (blocks, now, later, disp0, disp, vel, mass_b, coeff, place)
    full_rows((rows - HB) * (1 - rep), HB, *state, out_a)
    full_rows(HB, rows - 2 * HB - min(LATE, rows - 2 * HB), *state)
    for i in range(HB):
        r = (rows - HB) * rep + i
        disp[r] = disp[r] - joint(r, now, coeff)


def late_rows(*refs):
    place, blocks, disp0, now, later, disp, vel, mass_b, coeff = refs[-9:]
    rows = disp.shape[0]
    late = min(LATE, rows - 2 * HB)
    state = (blocks, now, later, disp0, disp, vel, mass_b, coeff.at[WINDOW - 1], place)
    full_rows(rows - HB - late, late, *state)


def main_rows(step, *refs):
    place, blocks, now, disp, vel, mass_b, turned, coeff, halo, later, out = refs[-11:]
    rows = disp.shape[0]
    coeff = coeff.at[step]
    side = 1 - lax.axis_index("rep")
    for j in range(HB):
        now[(rows + HB) * side + j] = halo[j]
    state = (blocks, now, later, None, disp, vel, mass_b, coeff, place)
    full_rows(HB * side, rows - HB, *state)
    for j in range(HB):
        out[j] = later[(rows - HB) * side + HB + j]
    each(HB, lambda i: near_part(i, blocks, now, place, coeff, disp))


def far_part(dense, halo, window):
    rows, width, lanes = halo.shape
    start, size = window
    start = start if lanes > size else 0
    seen = halo[:, :, start : start + size].reshape(rows * width, size)
    return jnp.dot(dense[...], seen, preferred_element_type=jnp.float32)


def edge_rows(window, *refs):
    dense, disp, vel, mass_b, halo, later, out = refs[-7:]
    rows, width, _ = disp.shape
    image = far_part(dense, halo, window)
    start = (rows - HB) * lax.axis_index("rep")
    for i in range(HB):
        part = image[i * width : (i + 1) * width]
        out[i] = finish_row(start + i, part, later, disp, vel, mass_b, window)


def row_copies(disp, vel, disp_out, vel_out, sem, start, count, g, window):
    at = (pl.ds(start, count), slice(None), pl.ds(*window))
    return [
        pltpu.make_async_copy(disp.at[at], disp_out.at[at], sem.at[0, g]),
        pltpu.make_async_copy(vel.at[at], vel_out.at[at], sem.at[1, g]),
    ]


def main_last(*refs):
    place, blocks, now, disp, vel, turned, coeff, halo, disp_out, vel_out, sem = refs[-11:]
    rows = disp.shape[0]
    coeff = coeff.at[0]
    side = 1 - lax.axis_index("rep")
    for j in range(HB):
        now[(rows + HB) * side + j] = halo[j]
    sent = []
    for g in range(rows // HB - 1):
        start = HB * side + g * HB

        def one(i):
            r = start + i
            image = product(blocks, now, place, r) + joint(r, now, coeff)
            finish_row(r, image, None, disp, vel, None)

        each(HB, one)
        copies = row_copies(disp, vel, disp_out, vel_out, sem, start, HB, g, (0, disp.shape[2]))
        sent += begin(copies)
    each(HB, lambda i: near_part(i, blocks, now, place, coeff, disp))
    end(sent)


def edge_last(window, *refs):
    dense, disp, vel, halo, disp_out, vel_out, sem = refs[-7:]
    rows, width, _ = disp.shape
    start = (rows - HB) * lax.axis_index("rep")
    image = far_part(dense, halo, window)
    for i in range(HB):
        part = image[i * width : (i + 1) * width]
        finish_row(start + i, part, None, disp, vel, None, window)
    end(begin(row_copies(disp, vel, disp_out, vel_out, sem, start, HB, 0, window)))


def body(adj_disp, adj_vel, tangent_blocks, block_cols, inv_mass, joint_stiff, contact, states):
    rows, width, lanes = adj_disp.shape
    ring = lax.axis_size(RING)
    total = rows * ring
    inner, outer = ring_pairs(ring)
    pieces = lax.axis_size("ckpt")
    f32, bf16 = jnp.float32, jnp.bfloat16
    vm = pl.BlockSpec(memory_space=pltpu.VMEM)
    sm = pl.BlockSpec(memory_space=pltpu.SMEM)
    hbm = pl.BlockSpec(memory_space=pltpu.HBM)
    like = lambda a: pltpu.VMEM(a.shape, a.dtype)
    edge_t = pltpu.VMEM((HB, width, lanes), bf16)
    ext = pltpu.VMEM((rows + 2 * HB + 1, width, lanes), bf16)
    full = pltpu.VMEM((rows, width, lanes), f32)
    table = pltpu.VMEM((rows, width), f32)
    upright = pltpu.VMEM((WINDOW, width, rows), f32)
    dma = pltpu.SemaphoreType.DMA
    light = pl.CostEstimate(flops=1000, bytes_accessed=1000, transcendentals=0)
    heavy = pl.CostEstimate(flops=4_000_000_000, bytes_accessed=1000, transcendentals=0)
    adj_disp, adj_vel, tangent_blocks, cols, inv_mass, joint_stiff, contact, mine = (
        pltpu.with_memory_space_constraint(a, pltpu.HBM)
        for a in (
            adj_disp, adj_vel, tangent_blocks, block_cols.T, inv_mass, joint_stiff, contact, states
        )
    )

    def call(kernel, name, held, given, specs, made, made_specs, scratch=(), cost=light):
        return pl.pallas_call(
            kernel,
            name=name,
            out_shape=tuple(like(a) for a in held) + tuple(made),
            in_specs=[vm] * len(held) + list(specs),
            out_specs=(vm,) * len(held) + tuple(made_specs),
            input_output_aliases={i: i for i in range(len(held))},
            scratch_shapes=list(scratch),
            compiler_params=pltpu.CompilerParams(vmem_limit_bytes=VMEM_LIMIT),
            cost_estimate=cost,
        )(*held, *given)

    windows = windows_of(lanes)
    edges_t = [pltpu.VMEM((HB, width, size), bf16) for _, size in windows]

    out_b, *out_a = call(
        head, "head", [], [adj_vel, inv_mass], [hbm] * 2, [edge_t] + edges_t,
        [vm] * (len(windows) + 1), [edge_t, edge_t, table, dma((3,))],
    )
    states_late, out_a = lax.optimization_barrier((states, out_a))
    halo_a = [lax.ppermute(a, RING, inner) for a in out_a]
    whole_b = lax.ppermute(out_b, RING, outer)
    halo_b = [whole_b] * len(windows)
    others = [
        lax.ppermute(states_late, "ckpt", [((i + j) % pieces, i) for i in range(pieces)])
        for j in range(1, pieces)
    ]

    blocks, disp0, now, disp, vel, mass_b, bent, turned, place, dense = call(
        functools.partial(load_all, total), "load_all", [],
        [tangent_blocks, adj_vel, adj_disp, inv_mass, joint_stiff, contact, mine, cols], [hbm] * 8,
        [
            like(tangent_blocks), like(adj_disp), ext, full, full,
            pltpu.VMEM((rows, width, 128), f32), upright, upright, like(cols),
            pltpu.VMEM((HB * width, HB * width), bf16),
        ],
        [vm] * 10,
        [
            like(adj_vel), like(cols), pltpu.SMEM(cols.shape, jnp.int32), table, table,
            pltpu.VMEM(contact.shape, jnp.int32), pltpu.VMEM(states.shape, f32), dma((12,)),
        ],
    )
    blocks, disp0, now, disp, vel, mass_b, _, turned, *_, later, coeff, out_a = call(
        functools.partial(first_step, pieces), "first_step",
        [blocks, disp0, now, disp, vel, mass_b, bent, turned] + halo_a + others, [place], [sm],
        [ext, pltpu.VMEM((WINDOW, rows, width, 128), f32), edge_t], [vm] * 3,
    )
    halo_a = lax.ppermute(out_a, RING, inner)
    for step in range(WINDOW - 1, 0, -1):
        if step < WINDOW - 1:
            blocks, later, disp, vel, mass_b, turned, coeff, _, now, out_a = call(
                functools.partial(main_rows, step), "main_rows",
                [blocks, later, disp, vel, mass_b, turned, coeff, halo_a, now],
                [place], [sm], [edge_t], [vm],
            )
            now, later = later, now
            halo_a = lax.ppermute(out_a, RING, inner)
        sent = []
        for n, window in enumerate(windows):
            dense, disp, vel, mass_b, halo, later, out = call(
                functools.partial(edge_rows, window), "edge_rows",
                [dense, disp, vel, mass_b, halo_b[n], later], [], [], [edges_t[n]], [vm],
                (), heavy if n else light,
            )
            sent.append(lax.ppermute(out, RING, outer))
            if step == WINDOW - 1:
                halo_b = [halo] * len(windows)
                if n == 0:
                    blocks, _, now, later, disp, vel, mass_b, coeff = call(
                        late_rows, "late_rows",
                        [blocks, disp0, now, later, disp, vel, mass_b, coeff], [place], [sm],
                        [], [],
                    )
        halo_b = sent

    shape = jax.ShapeDtypeStruct((rows, width, lanes), f32)
    *_, disp, vel, _, _, _, disp_out, vel_out = call(
        main_last, "main_last", [blocks, later, disp, vel, turned, coeff, halo_a], [place], [sm],
        [shape] * 2, [hbm] * 2, [dma((2, rows // HB - 1))],
    )
    for window, halo in zip(windows, halo_b):
        held = [dense, disp, vel, halo]
        dense, disp, vel, _, disp_out, vel_out = pl.pallas_call(
            functools.partial(edge_last, window),
            name="edge_last",
            out_shape=tuple(like(a) for a in held) + (shape,) * 2,
            in_specs=[vm] * 4 + [hbm] * 2,
            out_specs=(vm,) * 4 + (hbm,) * 2,
            input_output_aliases={i: i for i in range(6)},
            scratch_shapes=[dma((2, HB))],
            compiler_params=pltpu.CompilerParams(vmem_limit_bytes=VMEM_LIMIT),
            cost_estimate=light,
        )(*held, disp_out, vel_out)
    return disp_out, vel_out


def solution(mesh):
    placed = (
        P(("groups", "space", "rep"), None, "ckpt"),
        P(("groups", "space", "rep"), None, "ckpt"),
        P(("groups", "space", "rep"), None, None),
        P(("groups", "space", "rep"), None),
        P(("groups", "space", "rep"), None),
        P(("groups", "space", "rep"), None),
        P(None, ("groups", "space", "rep")),
        P(None, ("groups", "space", "rep"), "ckpt"),
    )
    return jax.shard_map(
        body,
        mesh=mesh,
        in_specs=placed,
        out_specs=(
            P(("groups", "space", "rep"), None, "ckpt"),
            P(("groups", "space", "rep"), None, "ckpt"),
        ),
        check_vma=False,
    )
```
